256 devices in a mesh: hier: 8 (over z), row: 32 (over x, y, core).
Axes of the slice: x: 4, y: 4, z: 8, core: 2. Of those that a mesh axis runs over, the one named last changes fastest.
Arguments:
- density: float32 [2, 16, 512, 512], P(None, 'hier', 'row')
- hamiltonian: float32 [512, 512], P('row')
- couplings: float32 [8, 512], replicated, may hold values from -5 to 5
- decay_rates: float32 [8], replicated, may hold values from 0.1 to 1
- bath_coeffs: float32 [2, 8], replicated, may hold values from 0.3 to 1.2
- levels: int32 [16, 8], replicated, may hold values from 0 to 2, as said below
- neighbours: int32 [2, 16, 8], replicated, may hold values from -1 to 15, as said below
Outputs:
- evolved: float32 [2, 16, 512, 512], P(None, 'hier', 'row')
The draws below stay inside these ranges and needn't reach their ends.
Inputs may be any that keep to these rules, and one draw needn't show every extreme that they name: levels[m, k] counts the excitations of mode k in matrix m; the kept set holds the vector of zeros, then unit vectors, then vectors of total two, stored in an order drawn from the seed. neighbours[0, m, k] is the index of the kept matrix whose levels are those of m plus one in mode k, neighbours[1, m, k] the one with one less, -1 where that matrix is not kept.
All inputs are finite; a program needn't handle non-finite values.
Results may differ from the reference program's by a relative error of at most 0.0001.
Values sent between devices are 32-bit elements; how exact they have to be, the bound alone decides.
No kernel may reach another device: no remote copies, remote signals or barrier semaphores. Data moves between devices by JAX's collectives and lax.ppermute only.
A program may use at most 64 MiB of HBM per device.

```python
import math
import jax
import jax.numpy as jnp
import numpy as np
from jax import lax

N = 512
K = 8
STEPS = 1
TERMS = 3
MATRICES = 16


def build_hierarchy(key):
    base = jax.random.fold_in(key, 7)
    pairs = K * (K + 1) // 2
    table = np.zeros((1 + K + pairs, K), np.int32)
    for first in range(K):
        table[1 + first, first] = 1
    position = 1 + K
    for first in range(K):
        for second in range(first, K):
            table[position, first] += 1
            table[position, second] += 1
            position += 1
    tail = jax.random.permutation(jax.random.fold_in(base, 1), pairs).astype(jnp.int32) + 1 + K
    order_list = jnp.concatenate([jnp.arange(1 + K, dtype=jnp.int32), tail])[:MATRICES]
    chosen = jnp.asarray(table)[order_list]
    storage = jax.random.permutation(jax.random.fold_in(base, 2), MATRICES)
    stored = chosen[storage]
    unit = jnp.eye(K, dtype=jnp.int32)
    upward = stored[:, None, :] + unit[None]
    downward = stored[:, None, :] - unit[None]
    labels = jnp.arange(MATRICES, dtype=jnp.int32) + 1

    def locate(target):
        match = jnp.all(target[:, :, None, :] == stored[None, None, :, :], axis=-1).astype(jnp.int32)
        return jnp.sum(match * labels, axis=-1) - 1
    return (stored, jnp.stack([locate(upward), locate(downward)]))


def draw_levels(key, part):
    return build_hierarchy(key)[0]


def draw_neighbours(key, part):
    return build_hierarchy(key)[1]


def draw_density(key, part):
    base = jax.random.fold_in(key, 11)
    raw = jax.random.normal(base, (2, MATRICES, N, N), jnp.float32)
    real_part = (raw[0] + jnp.swapaxes(raw[0], 1, 2)) * 0.7071
    imag_part = (raw[1] - jnp.swapaxes(raw[1], 1, 2)) * 0.7071
    return jnp.stack([real_part, imag_part])


def draw_hamiltonian(key, part):
    base = jax.random.fold_in(key, 13)
    raw = jax.random.normal(base, (N, N), jnp.float32)
    energies = jax.random.uniform(jax.random.fold_in(base, 1), (N,), jnp.float32, -1.0, 1.0)
    spread = 1.0
    return (raw + raw.T) * (spread / (2.0 * N) ** 0.5) + jnp.diag(energies)


def shard_levels(stream_key, dims, split, low, high):
    loudness, own = 1.0, jax.random.fold_in(stream_key, 6)
    for dim, parts in split:
        heights = jnp.exp(jax.random.uniform(jax.random.fold_in(own, dim), (parts,), jnp.float32, low / len(split), high / len(split)))
        loudness = loudness * jnp.repeat(heights, dims[dim] // parts).reshape([-1 if axis == dim else 1 for axis in range(len(dims))])
    return loudness


def normal_values(own_key, extent, width, most, held_as=jnp.bfloat16):
    drawn = jax.random.normal(own_key, extent, jnp.float32) * width
    return jnp.minimum(jnp.maximum(drawn, -most), most).astype(held_as)


def setup_inputs(seed: int = 0) -> dict:
    key_of = jax.random.split(jax.random.key(seed), 8)
    density = draw_density(jax.random.fold_in(key_of[7], 71), 0)
    hamiltonian = draw_hamiltonian(jax.random.fold_in(key_of[7], 71), 0)
    couplings = normal_values(key_of[2], (K, N), 1.0, 5.0, jnp.float32)
    decay_rates = jnp.clip(jnp.exp(jax.random.uniform(key_of[3], (K,), jnp.float32, math.log(0.1), math.log(1.0))), 0.1, 1.0)
    bath_coeffs = jnp.clip(jax.random.uniform(key_of[4], (2, K), jnp.float32, 0.3, 1.2), 0.3, 1.2)
    levels = draw_levels(jax.random.fold_in(key_of[7], 71), 0)
    neighbours = draw_neighbours(jax.random.fold_in(key_of[7], 71), 0)
    return {"density": density, "hamiltonian": hamiltonian, "couplings": couplings, "decay_rates": decay_rates, "bath_coeffs": bath_coeffs, "levels": levels, "neighbours": neighbours}


time_step = 0.25
exact_precision = lax.Precision.HIGHEST


def couple(plus_rows, minus_rows, level_rows, real_part, imag_part, source_first, couplings, bath_coeffs, row_first):
    source_count = real_part.shape[0]
    row_count = real_part.shape[1]
    source_ids = source_first + jnp.arange(source_count, dtype=jnp.int32)
    plus_hits = (plus_rows[:, None, :] == source_ids[None, :, None]).astype(jnp.float32)
    minus_hits = (minus_rows[:, None, :] == source_ids[None, :, None]).astype(jnp.float32)
    minus_hits = minus_hits * level_rows[:, None, :].astype(jnp.float32)
    odd_weights = plus_hits + minus_hits * bath_coeffs[0]
    even_weights = minus_hits * bath_coeffs[1]
    odd_field = jnp.einsum('mjk,kn->mjn', odd_weights, couplings, precision=exact_precision)
    even_field = jnp.einsum('mjk,kn->mjn', even_weights, couplings, precision=exact_precision)
    odd_rows = lax.dynamic_slice_in_dim(odd_field, row_first, row_count, 2)
    even_rows = lax.dynamic_slice_in_dim(even_field, row_first, row_count, 2)
    real_out = (jnp.einsum('mja,jab->mab', even_rows, real_part, precision=exact_precision)
                + jnp.einsum('mjb,jab->mab', even_field, real_part, precision=exact_precision)
                + jnp.einsum('mja,jab->mab', odd_rows, imag_part, precision=exact_precision)
                - jnp.einsum('mjb,jab->mab', odd_field, imag_part, precision=exact_precision))
    imag_out = (jnp.einsum('mja,jab->mab', even_rows, imag_part, precision=exact_precision)
                + jnp.einsum('mjb,jab->mab', even_field, imag_part, precision=exact_precision)
                - jnp.einsum('mja,jab->mab', odd_rows, real_part, precision=exact_precision)
                + jnp.einsum('mjb,jab->mab', odd_field, real_part, precision=exact_precision))
    return jnp.stack([real_out, imag_out])


def reference(density, hamiltonian, couplings, decay_rates, bath_coeffs, levels, neighbours):
    damping = jnp.dot(levels.astype(jnp.float32), decay_rates, precision=exact_precision)
    sites_count = hamiltonian.shape[0]

    def liouville(current):
        product = jnp.dot(current.reshape(-1, sites_count), hamiltonian, precision=exact_precision,
                          preferred_element_type=jnp.float32).reshape(current.shape)
        conjugated = jnp.swapaxes(product, 2, 3)
        coherent = jnp.stack([-conjugated[1] - product[1], product[0] - conjugated[0]])
        ladder = couple(neighbours[0], neighbours[1], levels, current[0], current[1], 0,
                        couplings, bath_coeffs, 0)
        return coherent - damping[None, :, None, None] * current + ladder

    current = density
    for step_index in range(STEPS):
        increment = current
        summed = current
        for order_index in range(1, TERMS + 1):
            increment = (time_step / order_index) * liouville(increment)
            summed = summed + increment
        current = summed
    return current
```

```python
import functools

import jax
import jax.numpy as jnp
from jax import lax
from jax.experimental import pallas as pl
from jax.experimental.pallas import tpu as pltpu
from jax.sharding import PartitionSpec as P

time_step = 0.25
A1 = time_step
A2 = A1 * time_step / 2
A3 = A2 * time_step / 3

PLANES = 8
ROWS = 32
EDGES = 264


VMEM = pl.BlockSpec(memory_space=pltpu.VMEM)
SMEM = pl.BlockSpec(memory_space=pltpu.SMEM)


def f32(*shape):
    return jax.ShapeDtypeStruct(shape, jnp.float32)


def split_kernel(pos, density, *refs):
    slots, tiles = refs[:8], refs[8]
    plane = pos[0]
    for p in range(4):
        for j in range(4):
            tiles[pl.ds(64 * p + 16 * j, 16), :] = density[p, :, 128 * j : 128 * j + 128]
    for s in range(PLANES):
        first = 2 * ((plane + s) & 7)
        for a in range(2):
            picked = tiles[pl.ds(first + a, 16, stride=16), :]
            for p in range(4):
                slots[s][8 * p + 4 * a : 8 * p + 4 * a + 4, :] = picked[4 * p : 4 * p + 4]


def prepare_kernel(pos, levels, neighbours, decay, bath, couplings, ints, floats, fields):
    plane = pos[0]
    row = pos[1]

    def place(g):
        return ((plane - g // 2) & 7) * 4 + (g & 1)

    def scan(direction, count):
        def step(i, count):
            m = i // 8
            k = i % 8
            other = neighbours[direction, m, k]
            ints[0, count] = place(m)
            ints[1, count] = place(jnp.maximum(other, 0))
            ints[2, count] = k
            if direction == 0:
                floats[0, count] = 0.0
                floats[1, count] = 1.0
            else:
                level = levels[m, k].astype(jnp.float32)
                floats[0, count] = level * bath[1, k]
                floats[1, count] = level * bath[0, k]
            return count + (other >= 0).astype(jnp.int32)

        return lax.fori_loop(0, 128, step, count)

    count = scan(1, scan(0, 0))
    ints[3, 0] = count
    for m in range(16):
        total = levels[m, 0].astype(jnp.float32) * decay[0]
        for k in range(1, 8):
            total = total + levels[m, k].astype(jnp.float32) * decay[k]
        floats[2, place(m)] = total

    values = couplings[...]
    lane = lax.broadcasted_iota(jnp.int32, values.shape, 1)
    for a in range(2):
        own = jnp.sum(jnp.where(lane == row + a, values, 0.0), axis=1, keepdims=True)
        own = jnp.broadcast_to(own, (8, 128))
        for j in range(4):
            here = pl.ds(4 * a + j, 8, stride=8)
            there = values[:, 128 * j : 128 * j + 128]
            fields[0, here, :] = own - there
            fields[1, here, :] = own + there
            fields[2, here, :] = there


def mix(ints, floats, fields, source, both, right):
    def step(e, carry):
        m = ints[0, e]
        j = ints[1, e]
        k = pl.multiple_of(ints[2, e] * 8, 8)
        even = floats[0, e]
        odd = floats[1, e]
        x = source[j]
        y = source[j + 2]
        if both is not None:
            f = odd * fields[0, pl.ds(k, 8), :]
            g = even * fields[1, pl.ds(k, 8), :]
            both[m] = both[m] + (g * x + f * y)
            both[m + 2] = both[m + 2] + (g * y - f * x)
        if right is not None:
            c = fields[2, pl.ds(k, 8), :]
            g = even * c
            f = odd * c
            right[m] = right[m] + (g * x - f * y)
            right[m + 2] = right[m + 2] + (g * y + f * x)
        return carry

    lax.fori_loop(0, ints[3, 0], step, 0)


def decayed(floats, source, scale=-1.0):
    parts = []
    for s in range(PLANES):
        for part in range(2):
            for m in range(2):
                parts.append((scale * floats[2, 4 * s + m]) * source[4 * s + 2 * part + m])
    return jnp.stack(parts)


def early_kernel(ints, floats, fields, *refs):
    slots, (state, first, right, second) = refs[:8], refs[8:]
    for s in range(PLANES):
        state[4 * s : 4 * s + 4] = slots[s][...].reshape(4, 8, 128)
    first[...] = decayed(floats, state)
    right[...] = jnp.zeros_like(right)
    mix(ints, floats, fields, state, first, right)
    first[...] = A2 * state[...] + A3 * first[...]
    second[...] = decayed(floats, first)
    mix(ints, floats, fields, first, second, None)


def gather_rows(ref):
    return jnp.concatenate(
        [
            jnp.concatenate([ref[pl.ds(4 * a + j, 32, stride=8), :] for j in range(4)], axis=1)
            for a in range(2)
        ],
        axis=0,
    )


def spread_rows(ref, value):
    for a in range(2):
        for j in range(4):
            ref[pl.ds(4 * a + j, 32, stride=8), :] = value[
                32 * a : 32 * a + 32, 128 * j : 128 * j + 128
            ]


def halves(value):
    high = value.astype(jnp.bfloat16)
    low = (value - high.astype(jnp.float32)).astype(jnp.bfloat16)
    return high, low


def times_i(value):
    value = value.reshape(PLANES, 2, 2, 8, 128)
    return jnp.concatenate([-value[:, 1:], value[:, :1]], axis=1).reshape(32, 8, 128)


def swap_blocks(value):
    lead = value.shape[0]
    block = lax.broadcasted_iota(jnp.int32, (8, 128), 1) // 16
    for k in range(3):
        width = 16 << k
        low = ((block >> k) & 1) == 0
        pairs = value.reshape(lead, 4 >> k, 2, 1 << k, 8, 128)
        zero, one = pairs[:, :, 0], pairs[:, :, 1]
        shape = zero.shape
        zero = zero.reshape(-1, 128)
        one = one.reshape(-1, 128)
        up = pltpu.roll(one, width, 1)
        down = pltpu.roll(zero, 128 - width, 1)
        low = jnp.broadcast_to(low[None], (zero.shape[0] // 8, 8, 128)).reshape(-1, 128)
        new_zero = jnp.where(low, zero, up).reshape(shape)
        new_one = jnp.where(low, down, one).reshape(shape)
        value = jnp.stack([new_zero, new_one], axis=2).reshape(lead, 8, 8, 128)
    return value


def rows_kernel(
    pos, ints, floats, fields, h, state, right, first, second,
    message, h_high, h_low, rows, p, ep, bp,
):
    plane = pos[0]
    high, low = halves(h[...])
    h_high[...] = high
    h_low[...] = low

    def product(value):
        count = value.shape[0]
        value_high, value_low = halves(value)
        main = jnp.dot(
            jnp.concatenate([value_high, value_low], axis=0),
            high,
            preferred_element_type=jnp.float32,
        )
        rest = jnp.dot(value_high, low, preferred_element_type=jnp.float32)
        return main[:count] + main[count:] + rest

    def apply(values):
        stacked = []
        for value in values:
            rows[...] = value.reshape(256, 128)
            stacked.append(gather_rows(rows))
        result = product(jnp.concatenate(stacked, axis=0))
        out = []
        for i in range(len(values)):
            spread_rows(rows, result[64 * i : 64 * i + 64])
            out.append(times_i(rows[...].reshape(32, 8, 128)))
        return out

    s_value = state[...]
    (p_value,) = apply([s_value])
    p[...] = p_value
    v1, edge = apply([first[...] + A3 * p_value, p_value + right[...]])
    damped = decayed(floats, p)
    ep[...] = damped
    bp[...] = damped + edge
    mix(ints, floats, fields, p, ep, bp)
    k_value = A2 * p_value + 3 * A3 * bp[...]
    z_value = 0.5 * A1 * s_value + v1 + A3 * ep[...] + 0.5 * second[...]
    v2 = z_value + 0.5 * A1 * s_value + 0.5 * second[...]
    (g_value,) = apply([v2])
    p[...] = z_value
    ep[...] = g_value + decayed(floats, p)
    mix(ints, floats, fields, p, ep, None)
    both = jnp.concatenate(
        [k_value.reshape(8, 4, 8, 128), ep[...].reshape(8, 4, 8, 128)], axis=1
    )
    both = swap_blocks(both)
    for s in range(PLANES):
        start = 2 * ((plane - s) & 7)
        for b in range(8):
            for a in range(2):
                message[pl.ds(start + 16 * b + a, 4, stride=128), :] = both[
                    s, b, 4 * a : 4 * a + 4, :
                ]


def columns_kernel(received, h_high, h_low, message, total):
    value = received[...]
    high, low = halves(value)
    main = jnp.dot(
        h_high[...], jnp.concatenate([high, low], axis=1), preferred_element_type=jnp.float32
    )
    rest = jnp.dot(h_low[...], high, preferred_element_type=jnp.float32)
    z = main[:, :128] + main[:, 128:] + rest
    lane = lax.broadcasted_iota(jnp.int32, z.shape, 1)
    other = pltpu.roll(value, 64, 1)
    result = jnp.where(
        lane < 32, pltpu.roll(z, 96, 1) + other, pltpu.roll(z, 32, 1) - other
    )
    total[...] = result
    tiles = result.reshape(32, 2, 8, 128)
    upper = pltpu.roll(tiles[:, 1].reshape(256, 128), 64, 1)
    lane = lax.broadcasted_iota(jnp.int32, upper.shape, 1)
    message[...] = jnp.where(lane < 64, tiles[:, 0].reshape(256, 128), upper)


def base_kernel(density, total, base):
    base[...] = density[...] + jnp.transpose(total[...])[:64]


def finish_kernel(base, received, out):
    value = swap_blocks(received[...].reshape(4, 8, 8, 128))
    for g in range(4):
        for half in range(2):
            for p in range(4):
                row = slice(16 * p + 8 * half, 16 * p + 8 * half + 8)
                col = slice(128 * g, 128 * g + 128)
                part = value[g, 4 * half + p]
                out[row, col] = base[row, col] + part if p < 2 else base[row, col] - part


def on_device(density, hamiltonian, couplings, decay_rates, bath_coeffs, levels, neighbours):
    plane = lax.axis_index("hier").astype(jnp.int32)
    group = lax.axis_index("row").astype(jnp.int32)
    pos = jnp.stack([plane, 16 * group + 2 * plane])

    full_h = lax.all_to_all(
        jnp.broadcast_to(hamiltonian[None], (ROWS, 16, 512)), "row", 0, 0, tiled=True
    ).reshape(512, 512)
    slots = pl.pallas_call(
        split_kernel,
        out_shape=[f32(32, 128)] * 8,
        in_specs=[SMEM, VMEM],
        out_specs=[VMEM] * 8,
        scratch_shapes=[pltpu.VMEM((256, 128), jnp.float32)],
        name="split",
    )(pos, density.reshape(4, 16, 512))
    arrived = [slots[0]] + [None] * 7
    for s in (1, 7, 2, 6, 3, 5, 4):
        pairs = [(i, (i + s) % PLANES) for i in range(PLANES)]
        arrived[s] = lax.ppermute(slots[s], "hier", pairs)

    ints, floats, fields = pl.pallas_call(
        prepare_kernel,
        out_shape=[jax.ShapeDtypeStruct((4, EDGES), jnp.int32), f32(3, EDGES), f32(3, 64, 128)],
        in_specs=[SMEM] * 5 + [VMEM],
        out_specs=[SMEM, SMEM, VMEM],
        name="prepare",
    )(pos, levels, neighbours, decay_rates, bath_coeffs, couplings)

    state, first, right, second = pl.pallas_call(
        early_kernel,
        out_shape=[f32(32, 8, 128)] * 4,
        in_specs=[SMEM, SMEM] + [VMEM] * 9,
        out_specs=[VMEM] * 4,
        name="early",
    )(ints, floats, fields, *arrived)

    bf16 = jax.ShapeDtypeStruct((512, 512), jnp.bfloat16)
    message, h_high, h_low = pl.pallas_call(
        rows_kernel,
        out_shape=[f32(512, 128), bf16, bf16],
        in_specs=[SMEM] * 3 + [VMEM] * 6,
        out_specs=[VMEM] * 3,
        scratch_shapes=[pltpu.VMEM((256, 128), jnp.float32)]
        + [pltpu.VMEM((32, 8, 128), jnp.float32)] * 3,
        name="rows",
    )(pos, ints, floats, fields, full_h, state, right, first, second)

    received = lax.all_to_all(
        message.reshape(256, 2, 128), ("row", "hier"), 0, 0, tiled=True
    ).reshape(512, 128)

    message, total = pl.pallas_call(
        columns_kernel,
        out_shape=[f32(256, 128), f32(512, 128)],
        in_specs=[VMEM] * 3,
        out_specs=[VMEM] * 2,
        name="columns",
    )(received, h_high, h_low)

    received = lax.all_to_all(
        message.reshape(ROWS, 8, 128), "row", 0, 0, tiled=True
    ).reshape(256, 128)

    base = pl.pallas_call(
        base_kernel, out_shape=f32(64, 512), in_specs=[VMEM] * 2, out_specs=VMEM, name="base"
    )(density.reshape(64, 512), total)
    out = pl.pallas_call(
        finish_kernel, out_shape=f32(64, 512), in_specs=[VMEM] * 2, out_specs=VMEM, name="finish"
    )(base, received)
    return out.reshape(2, 2, 16, 512)


def solution(mesh):
    in_specs = (P(None, "hier", "row", None), P("row", None), P(), P(), P(), P(), P())
    out_specs = P(None, "hier", "row", None)
    return jax.shard_map(
        on_device, mesh=mesh, in_specs=in_specs, out_specs=out_specs, check_vma=False
    )
```

```python
import functools

import jax
import jax.numpy as jnp
from jax import lax
from jax.experimental import pallas as pl
from jax.experimental.pallas import tpu as pltpu
from jax.sharding import PartitionSpec as P

time_step = 0.25
A1 = time_step
A2 = A1 * time_step / 2
A3 = A2 * time_step / 3

PLANES = 8
ROWS = 32
EDGES = 264


VMEM = pl.BlockSpec(memory_space=pltpu.VMEM)
SMEM = pl.BlockSpec(memory_space=pltpu.SMEM)


def f32(*shape):
    return pltpu.VMEM(shape, jnp.float32)


def near(*arrays):
    return [pltpu.with_memory_space_constraint(array, pltpu.VMEM) for array in arrays]


def my_plane():
    return lax.axis_index("hier").astype(jnp.int32)


def split_kernel(density, hamiltonian, *refs):
    copies, slots, tiles = refs[0], refs[1:9], refs[9]
    plane = my_plane()
    own = hamiltonian[...]
    for r in range(ROWS):
        copies[r] = own
    for p in range(4):
        for j in range(4):
            tiles[pl.ds(64 * p + 16 * j, 16), :] = density[p, :, 128 * j : 128 * j + 128]
    for s in range(PLANES):
        first = 2 * ((plane + s) & 7)
        for a in range(2):
            picked = tiles[pl.ds(first + a, 16, stride=16), :]
            for p in range(4):
                slots[s][8 * p + 4 * a : 8 * p + 4 * a + 4, :] = picked[4 * p : 4 * p + 4]


def prepare_kernel(levels, neighbours, decay, bath, couplings, ints, floats, fields):
    plane = my_plane()
    row = 16 * lax.axis_index("row").astype(jnp.int32) + 2 * plane
    decays = [decay[k] for k in range(8)]
    evens = [bath[1, k] for k in range(8)]
    odds = [bath[0, k] for k in range(8)]

    def place(g):
        return ((plane - (g >> 1)) & 7) * 4 + (g & 1)

    def scan(m, count):
        here = place(m)
        total = 0.0
        for k in range(8):
            level = levels[k, m].astype(jnp.float32)
            total = total + level * decays[k]
            other = neighbours[k, m]
            ints[0, count] = here
            ints[1, count] = place(other & 15)
            ints[2, count] = 8 * k
            floats[0, count] = level * evens[k]
            floats[1, count] = level * odds[k]
            count = count + (other >= 0).astype(jnp.int32)
        floats[2, here] = total
        return count

    ints[3, 0] = lax.fori_loop(0, 16, scan, 0)

    values = couplings[...]
    lane = lax.broadcasted_iota(jnp.int32, values.shape, 1)
    for a in range(2):
        own = jnp.sum(jnp.where(lane == row + a, values, 0.0), axis=1, keepdims=True)
        own = jnp.broadcast_to(own, (8, 128))
        for j in range(4):
            here = pl.ds(4 * a + j, 8, stride=8)
            there = values[:, 128 * j : 128 * j + 128]
            fields[0, here, :] = own - there
            fields[1, here, :] = own + there
            fields[2, here, :] = there


def mix(ints, floats, fields, source, both, right):
    def step(e, carry):
        m = ints[0, e]
        q = ints[1, e]
        k = pl.multiple_of(ints[2, e], 8)
        even = floats[0, e]
        odd = floats[1, e]
        xm, ym = source[m], source[m + 2]
        xq, yq = source[q], source[q + 2]
        if both is not None:
            d = fields[0, pl.ds(k, 8), :]
            f = odd * d
            g = even * fields[1, pl.ds(k, 8), :]
            both[m] = both[m] + (g * xq + f * yq)
            both[m + 2] = both[m + 2] + (g * yq - f * xq)
            both[q] = both[q] + d * ym
            both[q + 2] = both[q + 2] - d * xm
        if right is not None:
            c = fields[2, pl.ds(k, 8), :]
            g = even * c
            f = odd * c
            right[m] = right[m] + (g * xq - f * yq)
            right[m + 2] = right[m + 2] + (g * yq + f * xq)
            right[q] = right[q] - c * ym
            right[q + 2] = right[q + 2] + c * xm
        return carry

    lax.fori_loop(0, ints[3, 0], step, 0)


def decayed(floats, source):
    parts = []
    for s in range(PLANES):
        for part in range(2):
            for m in range(2):
                parts.append((-floats[2, 4 * s + m]) * source[4 * s + 2 * part + m])
    return jnp.stack(parts)


def early_kernel(ints, floats, fields, *refs):
    slots, (state, first, right, second) = refs[:8], refs[8:]
    for s in range(PLANES):
        state[4 * s : 4 * s + 4] = slots[s][...].reshape(4, 8, 128)
    first[...] = decayed(floats, state)
    right[...] = jnp.zeros_like(right)
    mix(ints, floats, fields, state, first, right)
    first[...] = A2 * state[...] + A3 * first[...]
    second[...] = decayed(floats, first)
    mix(ints, floats, fields, first, second, None)


def gather_rows(ref):
    return jnp.concatenate(
        [
            jnp.concatenate([ref[pl.ds(4 * a + j, 32, stride=8), :] for j in range(4)], axis=1)
            for a in range(2)
        ],
        axis=0,
    )


def spread_rows(ref, value):
    for a in range(2):
        for j in range(4):
            ref[pl.ds(4 * a + j, 32, stride=8), :] = value[
                32 * a : 32 * a + 32, 128 * j : 128 * j + 128
            ]


def halves(value):
    high = value.astype(jnp.bfloat16)
    low = (value - high.astype(jnp.float32)).astype(jnp.bfloat16)
    return high, low


def times_i(value):
    value = value.reshape(PLANES, 2, 2, 8, 128)
    return jnp.concatenate([-value[:, 1:], value[:, :1]], axis=1).reshape(32, 8, 128)


def swap_blocks(value):
    lead = value.shape[0]
    block = lax.broadcasted_iota(jnp.int32, (8, 128), 1) // 16
    for k in range(3):
        width = 16 << k
        low = ((block >> k) & 1) == 0
        pairs = value.reshape(lead, 4 >> k, 2, 1 << k, 8, 128)
        zero, one = pairs[:, :, 0], pairs[:, :, 1]
        shape = zero.shape
        zero = zero.reshape(-1, 128)
        one = one.reshape(-1, 128)
        up = pltpu.roll(one, width, 1)
        down = pltpu.roll(zero, 128 - width, 1)
        low = jnp.broadcast_to(low[None], (zero.shape[0] // 8, 8, 128)).reshape(-1, 128)
        new_zero = jnp.where(low, zero, up).reshape(shape)
        new_one = jnp.where(low, down, one).reshape(shape)
        value = jnp.stack([new_zero, new_one], axis=2).reshape(lead, 8, 8, 128)
    return value


def rows_kernel(
    ints, floats, fields, h, state, right, first, second,
    message, h_high, h_low, rows, p, ep, bp,
):
    plane = my_plane()
    high, low = halves(h[...])
    h_high[...] = high
    h_low[...] = low

    def product(value):
        count = value.shape[0]
        value_high, value_low = halves(value)
        main = jnp.dot(
            jnp.concatenate([value_high, value_low], axis=0),
            high,
            preferred_element_type=jnp.float32,
        )
        rest = jnp.dot(value_high, low, preferred_element_type=jnp.float32)
        return main[:count] + main[count:] + rest

    def apply(values):
        stacked = []
        for value in values:
            rows[...] = value.reshape(256, 128)
            stacked.append(gather_rows(rows))
        result = product(jnp.concatenate(stacked, axis=0))
        out = []
        for i in range(len(values)):
            spread_rows(rows, result[64 * i : 64 * i + 64])
            out.append(times_i(rows[...].reshape(32, 8, 128)))
        return out

    s_value = state[...]
    (p_value,) = apply([s_value])
    p[...] = p_value
    v1, edge = apply([first[...] + A3 * p_value, p_value + right[...]])
    damped = decayed(floats, p)
    ep[...] = damped
    bp[...] = damped + edge
    mix(ints, floats, fields, p, ep, bp)
    k_value = A2 * p_value + 3 * A3 * bp[...]
    z_value = 0.5 * A1 * s_value + v1 + A3 * ep[...] + 0.5 * second[...]
    v2 = z_value + 0.5 * A1 * s_value + 0.5 * second[...]
    (g_value,) = apply([v2])
    p[...] = z_value
    ep[...] = g_value + decayed(floats, p)
    mix(ints, floats, fields, p, ep, None)
    both = jnp.concatenate(
        [k_value.reshape(8, 4, 8, 128), ep[...].reshape(8, 4, 8, 128)], axis=1
    )
    both = swap_blocks(both)
    for s in range(PLANES):
        start = 2 * ((plane - s) & 7)
        for b in range(8):
            for a in range(2):
                message[pl.ds(start + 16 * b + a, 4, stride=128), :] = both[
                    s, b, 4 * a : 4 * a + 4, :
                ]


def columns_kernel(received, h_high, h_low, message, total):
    value = received[...]
    high, low = halves(value)
    main = jnp.dot(
        h_high[...], jnp.concatenate([high, low], axis=1), preferred_element_type=jnp.float32
    )
    rest = jnp.dot(h_low[...], high, preferred_element_type=jnp.float32)
    z = main[:, :128] + main[:, 128:] + rest
    lane = lax.broadcasted_iota(jnp.int32, z.shape, 1)
    other = pltpu.roll(value, 64, 1)
    result = jnp.where(
        lane < 32, pltpu.roll(z, 96, 1) + other, pltpu.roll(z, 32, 1) - other
    )
    total[...] = result
    tiles = result.reshape(32, 2, 8, 128)
    upper = pltpu.roll(tiles[:, 1].reshape(256, 128), 64, 1)
    lane = lax.broadcasted_iota(jnp.int32, upper.shape, 1)
    message[...] = jnp.where(lane < 64, tiles[:, 0].reshape(256, 128), upper)


def base_kernel(density, total, base):
    base[...] = density[...] + jnp.transpose(total[...])[:64]


def finish_kernel(base, received, out):
    value = swap_blocks(received[...].reshape(4, 8, 8, 128))
    for g in range(4):
        for half in range(2):
            for p in range(4):
                row = slice(16 * p + 8 * half, 16 * p + 8 * half + 8)
                col = slice(128 * g, 128 * g + 128)
                part = value[g, 4 * half + p]
                out[row, col] = base[row, col] + part if p < 2 else base[row, col] - part


def on_device(density, hamiltonian, couplings, decay_rates, bath_coeffs, levels, neighbours):
    copies, *slots = pl.pallas_call(
        split_kernel,
        out_shape=[f32(ROWS, 16, 512)] + [f32(32, 128)] * 8,
        in_specs=[VMEM] * 2,
        out_specs=[VMEM] * 9,
        scratch_shapes=[pltpu.VMEM((256, 128), jnp.float32)],
        name="split",
    )(density.reshape(4, 16, 512), hamiltonian)
    full_h = lax.all_to_all(copies, "row", 0, 0, tiled=True).reshape(512, 512)
    arrived = [slots[0]] + [None] * 7
    for s in (1, 7, 2, 6, 3, 5, 4):
        pairs = [(i, (i + s) % PLANES) for i in range(PLANES)]
        arrived[s] = lax.ppermute(slots[s], "hier", pairs)

    ints, floats, fields = pl.pallas_call(
        prepare_kernel,
        out_shape=[
            jax.ShapeDtypeStruct((4, EDGES), jnp.int32),
            jax.ShapeDtypeStruct((3, EDGES), jnp.float32),
            f32(3, 64, 128),
        ],
        in_specs=[SMEM] * 4 + [VMEM],
        out_specs=[SMEM, SMEM, VMEM],
        name="prepare",
    )(levels.T, neighbours[1].T, decay_rates, bath_coeffs, couplings)

    state, first, right, second = pl.pallas_call(
        early_kernel,
        out_shape=[f32(32, 8, 128)] * 4,
        in_specs=[SMEM, SMEM] + [VMEM] * 9,
        out_specs=[VMEM] * 4,
        name="early",
    )(ints, floats, *near(fields, *arrived))

    bf16 = pltpu.VMEM((512, 512), jnp.bfloat16)
    message, h_high, h_low = pl.pallas_call(
        rows_kernel,
        out_shape=[f32(512, 128), bf16, bf16],
        in_specs=[SMEM] * 2 + [VMEM] * 6,
        out_specs=[VMEM] * 3,
        scratch_shapes=[pltpu.VMEM((256, 128), jnp.float32)]
        + [pltpu.VMEM((32, 8, 128), jnp.float32)] * 3,
        name="rows",
    )(ints, floats, *near(fields, full_h, state, right, first, second))

    received = lax.all_to_all(
        message.reshape(256, 2, 128), ("row", "hier"), 0, 0, tiled=True
    ).reshape(512, 128)

    message, total = pl.pallas_call(
        columns_kernel,
        out_shape=[f32(256, 128), f32(512, 128)],
        in_specs=[VMEM] * 3,
        out_specs=[VMEM] * 2,
        name="columns",
    )(*near(received, h_high, h_low))

    received = lax.all_to_all(
        message.reshape(ROWS, 8, 128), "row", 0, 0, tiled=True
    ).reshape(256, 128)

    base = pl.pallas_call(
        base_kernel, out_shape=f32(64, 512), in_specs=[VMEM] * 2, out_specs=VMEM, name="base"
    )(density.reshape(64, 512), *near(total))
    out = pl.pallas_call(
        finish_kernel,
        out_shape=jax.ShapeDtypeStruct((64, 512), jnp.float32),
        in_specs=[VMEM] * 2,
        out_specs=VMEM,
        name="finish",
    )(*near(base, received))
    return out.reshape(2, 2, 16, 512)


def solution(mesh):
    in_specs = (P(None, "hier", "row", None), P("row", None), P(), P(), P(), P(), P())
    out_specs = P(None, "hier", "row", None)
    return jax.shard_map(
        on_device, mesh=mesh, in_specs=in_specs, out_specs=out_specs, check_vma=False
    )
```

```python
import jax
import jax.numpy as jnp
from jax import lax
from jax.experimental import pallas as pl
from jax.experimental.pallas import tpu as pltpu
from jax.sharding import PartitionSpec as P

time_step = 0.25
A1 = time_step
A2 = A1 * time_step / 2
A3 = A2 * time_step / 3

PLANES = 8
ROWS = 32
EDGES = 264


VMEM = pl.BlockSpec(memory_space=pltpu.VMEM)
ANY = pl.BlockSpec(memory_space=pl.ANY)
SMEM = pl.BlockSpec(memory_space=pltpu.SMEM)
PARAMS = pltpu.CompilerParams(vmem_limit_bytes=24 << 20)


def f32(*shape):
    return pltpu.VMEM(shape, jnp.float32)


def near(*arrays):
    return [pltpu.with_memory_space_constraint(array, pltpu.VMEM) for array in arrays]


def my_plane():
    return lax.axis_index("hier").astype(jnp.int32)


def split_kernel(density, hamiltonian, copies, near_blocks, far_blocks, rows, own, tiles, sems):
    plane = my_plane()
    group = lax.axis_index("row").astype(jnp.int32)
    fetch = pltpu.make_async_copy(density, rows, sems.at[0])
    fetch_own = pltpu.make_async_copy(hamiltonian, own, sems.at[1])
    fetch.start()
    fetch_own.start()
    fetch.wait()
    for p in range(4):
        for j in range(4):
            tiles[pl.ds(64 * p + 16 * j, 16), :] = rows[p, :, 128 * j : 128 * j + 128]
    for s in range(PLANES):
        first = 2 * (plane ^ s)
        target = far_blocks if s & 4 else near_blocks
        for a in range(2):
            picked = tiles[pl.ds(first + a, 16, stride=16), :]
            for p in range(4):
                target[s & 3, 8 * p + 4 * a : 8 * p + 4 * a + 4, :] = picked[4 * p : 4 * p + 4]
    fetch_own.wait()
    turned = pltpu.roll(own[...], (512 - 16 * group) & 511, 1)
    lane = lax.broadcasted_iota(jnp.int32, (16, 128), 1)
    main = jnp.where(lane < 16, 0.5 * turned[:, :128], turned[:, :128])
    last = 0.5 * turned[:, 256:384]
    lane = lax.broadcasted_iota(jnp.int32, (8, 128), 1)
    last = jnp.where(lane < 16, last[:8], pltpu.roll(last[8:], 16, 1))
    block = jnp.concatenate([main, turned[:, 128:256], last], axis=0)
    for r in range(ROWS):
        copies[r] = block


def join_symmetric(blocks, upper):
    lane = lax.broadcasted_iota(jnp.int32, (8, 128), 1)
    for r in range(ROWS):
        tile, offset = r // 8, 16 * (r % 8)
        for half in range(2):
            at = 8 * half
            first = blocks[r, at : at + 8, :]
            second = blocks[r, 16 + at : 24 + at, :]
            last = blocks[r, 32:40, :]
            if offset:
                first = pltpu.roll(first, offset, 1)
                second = pltpu.roll(second, offset, 1)
            if (offset - 16 * half) % 128:
                last = pltpu.roll(last, (offset - 16 * half) % 128, 1)
            last = jnp.where((lane >= offset) & (lane < offset + 16), last, 0.0)
            if offset:
                parts = [
                    jnp.where(lane >= offset, first, 0.0),
                    jnp.where(lane < offset, first, second),
                    jnp.where(lane < offset, second, last),
                ]
            else:
                parts = [first, second, last]
            parts.append(jnp.zeros_like(first))
            for i in range(4):
                col = 128 * ((tile + i) % 4)
                upper[16 * r + at : 16 * r + at + 8, col : col + 128] = parts[i]
    value = upper[...]
    return value + jnp.transpose(value)


def pack_kernel(near_blocks, far_blocks, *out):
    for s in range(1, 4):
        out[s - 1][0] = near_blocks[s]
        out[s - 1][1] = far_blocks[s]


def prepare(levels, neighbours, decay, bath, couplings, codes, ints, floats, fields):
    plane = my_plane()
    row = 16 * lax.axis_index("row").astype(jnp.int32) + 2 * plane

    def place(g):
        return (plane ^ (g >> 1)) * 4 + (g & 1)

    count = 0
    for m in range(16):
        for k in range(8):
            lower = neighbours[1, k, m]
            codes[count] = lower * 128 + (8 * m + k)
            count = count + (lower >= 0).astype(jnp.int32)
    ints[3, 0] = count

    def unpack(e, carry):
        code = codes[e]
        m = (code >> 3) & 15
        k = code & 7
        level = levels[k, m].astype(jnp.float32)
        ints[0, e] = place(m)
        ints[1, e] = place(code >> 7)
        ints[2, e] = 8 * k
        floats[0, e] = level * bath[1, k]
        floats[1, e] = level * bath[0, k]
        return carry

    lax.fori_loop(0, count, unpack, 0)
    for m in range(16):
        total = levels[0, m].astype(jnp.float32) * decay[0]
        for k in range(1, 8):
            total = total + levels[k, m].astype(jnp.float32) * decay[k]
        floats[2, place(m)] = total

    values = couplings[...]
    lane = lax.broadcasted_iota(jnp.int32, values.shape, 1)
    for a in range(2):
        own = jnp.sum(jnp.where(lane == row + a, values, 0.0), axis=1, keepdims=True)
        own = jnp.broadcast_to(own, (8, 128))
        for j in range(4):
            here = pl.ds(4 * a + j, 8, stride=8)
            there = values[:, 128 * j : 128 * j + 128]
            fields[0, here, :] = own - there
            fields[1, here, :] = own + there
            fields[2, here, :] = there


def mix(ints, floats, fields, source, both, right):
    def step(e, carry):
        m = ints[0, e]
        q = ints[1, e]
        k = pl.multiple_of(ints[2, e], 8)
        even = floats[0, e]
        odd = floats[1, e]
        xm, ym = source[m], source[m + 2]
        xq, yq = source[q], source[q + 2]
        if both is not None:
            d = fields[0, pl.ds(k, 8), :]
            f = odd * d
            g = even * fields[1, pl.ds(k, 8), :]
            both[m] = both[m] + (g * xq + f * yq)
            both[m + 2] = both[m + 2] + (g * yq - f * xq)
            both[q] = both[q] + d * ym
            both[q + 2] = both[q + 2] - d * xm
        if right is not None:
            c = fields[2, pl.ds(k, 8), :]
            g = even * c
            f = odd * c
            right[m] = right[m] + (g * xq - f * yq)
            right[m + 2] = right[m + 2] + (g * yq + f * xq)
            right[q] = right[q] - c * ym
            right[q + 2] = right[q + 2] + c * xm
        return carry

    lax.fori_loop(0, ints[3, 0], step, 0)


def decayed(floats, source):
    parts = []
    for s in range(PLANES):
        for part in range(2):
            for m in range(2):
                parts.append((-floats[2, 4 * s + m]) * source[4 * s + 2 * part + m])
    return jnp.stack(parts)


def gather_rows(ref):
    return jnp.concatenate(
        [
            jnp.concatenate([ref[pl.ds(4 * a + j, 32, stride=8), :] for j in range(4)], axis=1)
            for a in range(2)
        ],
        axis=0,
    )


def spread_rows(ref, value):
    for a in range(2):
        for j in range(4):
            ref[pl.ds(4 * a + j, 32, stride=8), :] = value[
                32 * a : 32 * a + 32, 128 * j : 128 * j + 128
            ]


def halves(value):
    high = value.astype(jnp.bfloat16)
    low = (value - high.astype(jnp.float32)).astype(jnp.bfloat16)
    return high, low


def times_i(value):
    value = value.reshape(PLANES, 2, 2, 8, 128)
    return jnp.concatenate([-value[:, 1:], value[:, :1]], axis=1).reshape(32, 8, 128)


def swap_blocks(value):
    lead = value.shape[0]
    block = lax.broadcasted_iota(jnp.int32, (8, 128), 1) // 16
    for k in range(3):
        width = 16 << k
        low = ((block >> k) & 1) == 0
        pairs = value.reshape(lead, 4 >> k, 2, 1 << k, 8, 128)
        zero, one = pairs[:, :, 0], pairs[:, :, 1]
        shape = zero.shape
        zero = zero.reshape(-1, 128)
        one = one.reshape(-1, 128)
        up = pltpu.roll(one, width, 1)
        down = pltpu.roll(zero, 128 - width, 1)
        low = jnp.broadcast_to(low[None], (zero.shape[0] // 8, 8, 128)).reshape(-1, 128)
        new_zero = jnp.where(low, zero, up).reshape(shape)
        new_one = jnp.where(low, down, one).reshape(shape)
        value = jnp.stack([new_zero, new_one], axis=2).reshape(lead, 8, 8, 128)
    return value


def rows_kernel(levels, neighbours, decay, bath, couplings, h, *refs):
    near_blocks, far_blocks, *pairs, message, h_high, h_low = refs[:8]
    codes, ints, floats, fields, state, first, right, second, rows, p, ep, bp, upper = refs[8:]
    plane = my_plane()
    prepare(levels, neighbours, decay, bath, couplings, codes, ints, floats, fields)
    high, low = halves(join_symmetric(h, upper))
    h_high[...] = high
    h_low[...] = low

    state[0:4] = near_blocks[0].reshape(4, 8, 128)
    state[16:20] = far_blocks[0].reshape(4, 8, 128)
    for s in range(1, 4):
        state[4 * s : 4 * s + 4] = pairs[s - 1][0].reshape(4, 8, 128)
        state[4 * s + 16 : 4 * s + 20] = pairs[s - 1][1].reshape(4, 8, 128)
    first[...] = decayed(floats, state)
    right[...] = jnp.zeros_like(right)
    mix(ints, floats, fields, state, first, right)
    first[...] = A2 * state[...] + A3 * first[...]
    second[...] = decayed(floats, first)
    mix(ints, floats, fields, first, second, None)

    def product(value):
        count = value.shape[0]
        value_high, value_low = halves(value)
        main = jnp.dot(
            jnp.concatenate([value_high, value_low], axis=0),
            high,
            preferred_element_type=jnp.float32,
        )
        rest = jnp.dot(value_high, low, preferred_element_type=jnp.float32)
        return main[:count] + main[count:] + rest

    def apply(values):
        stacked = []
        for value in values:
            rows[...] = value.reshape(256, 128)
            stacked.append(gather_rows(rows))
        result = product(jnp.concatenate(stacked, axis=0))
        out = []
        for i in range(len(values)):
            spread_rows(rows, result[64 * i : 64 * i + 64])
            out.append(times_i(rows[...].reshape(32, 8, 128)))
        return out

    s_value = state[...]
    (p_value,) = apply([s_value])
    p[...] = p_value
    v1, edge = apply([first[...] + A3 * p_value, p_value + right[...]])
    damped = decayed(floats, p)
    ep[...] = damped
    bp[...] = damped + edge
    mix(ints, floats, fields, p, ep, bp)
    k_value = A2 * p_value + 3 * A3 * bp[...]
    z_value = 0.5 * A1 * s_value + v1 + A3 * ep[...] + 0.5 * second[...]
    v2 = z_value + 0.5 * A1 * s_value + 0.5 * second[...]
    (g_value,) = apply([v2])
    p[...] = z_value
    ep[...] = g_value + decayed(floats, p)
    mix(ints, floats, fields, p, ep, None)
    both = jnp.concatenate(
        [k_value.reshape(8, 4, 8, 128), ep[...].reshape(8, 4, 8, 128)], axis=1
    )
    both = swap_blocks(both)
    for s in range(PLANES):
        start = 2 * (plane ^ s)
        for b in range(8):
            for a in range(2):
                message[pl.ds(start + 16 * b + a, 4, stride=128), :] = both[
                    s, b, 4 * a : 4 * a + 4, :
                ]


def columns_kernel(received, h_high, h_low, message, total):
    value = received[...]
    high, low = halves(value)
    main = jnp.dot(
        h_high[...], jnp.concatenate([high, low], axis=1), preferred_element_type=jnp.float32
    )
    rest = jnp.dot(h_low[...], high, preferred_element_type=jnp.float32)
    z = main[:, :128] + main[:, 128:] + rest
    lane = lax.broadcasted_iota(jnp.int32, z.shape, 1)
    other = pltpu.roll(value, 64, 1)
    result = jnp.where(
        lane < 32, pltpu.roll(z, 96, 1) + other, pltpu.roll(z, 32, 1) - other
    )
    total[...] = result
    tiles = result.reshape(32, 2, 8, 128)
    upper = pltpu.roll(tiles[:, 1].reshape(256, 128), 64, 1)
    lane = lax.broadcasted_iota(jnp.int32, upper.shape, 1)
    message[...] = jnp.where(lane < 64, tiles[:, 0].reshape(256, 128), upper)


def base_kernel(density, total, base):
    base[...] = density[...] + jnp.transpose(total[...])[:64]


def finish_kernel(base, received, out):
    value = swap_blocks(received[...].reshape(4, 8, 8, 128))
    for g in range(4):
        for half in range(2):
            for p in range(4):
                row = slice(16 * p + 8 * half, 16 * p + 8 * half + 8)
                col = slice(128 * g, 128 * g + 128)
                part = value[g, 4 * half + p]
                out[row, col] = base[row, col] + part if p < 2 else base[row, col] - part


def on_device(density, hamiltonian, couplings, decay_rates, bath_coeffs, levels, neighbours):
    copies, near_blocks, far_blocks = pl.pallas_call(
        split_kernel,
        out_shape=[f32(ROWS, 40, 128), f32(4, 32, 128), f32(4, 32, 128)],
        in_specs=[ANY] * 2,
        out_specs=[VMEM] * 3,
        scratch_shapes=[
            pltpu.VMEM((4, 16, 512), jnp.float32),
            pltpu.VMEM((16, 512), jnp.float32),
            pltpu.VMEM((256, 128), jnp.float32),
            pltpu.SemaphoreType.DMA((2,)),
        ],
        name="split",
        compiler_params=PARAMS,
    )(density.reshape(4, 16, 512), hamiltonian)
    blocks = lax.all_to_all(copies, "row", 0, 0, tiled=True)

    def swap(block, s):
        return lax.ppermute(block, "hier", [(i, i ^ s) for i in range(PLANES)])

    far_blocks = swap(far_blocks, 4)
    packed = pl.pallas_call(
        pack_kernel,
        out_shape=[f32(2, 32, 128)] * 3,
        in_specs=[VMEM] * 2,
        out_specs=[VMEM] * 3,
        name="pack",
        compiler_params=PARAMS,
    )(*near(near_blocks, far_blocks))
    pairs = [swap(packed[s - 1], s) for s in (1, 2, 3)]

    bf16 = pltpu.VMEM((512, 512), jnp.bfloat16)
    whole = pltpu.VMEM((32, 8, 128), jnp.float32)
    message, h_high, h_low = pl.pallas_call(
        rows_kernel,
        out_shape=[f32(512, 128), bf16, bf16],
        in_specs=[SMEM] * 4 + [VMEM] * 7,
        out_specs=[VMEM] * 3,
        scratch_shapes=[
            pltpu.SMEM((EDGES,), jnp.int32),
            pltpu.SMEM((4, EDGES), jnp.int32),
            pltpu.SMEM((3, EDGES), jnp.float32),
            pltpu.VMEM((3, 64, 128), jnp.float32),
            *[whole] * 4,
            pltpu.VMEM((256, 128), jnp.float32),
            *[whole] * 3,
            pltpu.VMEM((512, 512), jnp.float32),
        ],
        name="rows",
        compiler_params=PARAMS,
    )(
        levels.T,
        jnp.swapaxes(neighbours, 1, 2),
        decay_rates,
        bath_coeffs,
        couplings,
        *near(blocks, near_blocks, far_blocks, *pairs),
    )

    received = lax.all_to_all(
        message.reshape(256, 2, 128), ("row", "hier"), 0, 0, tiled=True
    ).reshape(512, 128)

    message, total = pl.pallas_call(
        columns_kernel,
        out_shape=[f32(256, 128), f32(512, 128)],
        in_specs=[VMEM] * 3,
        out_specs=[VMEM] * 2,
        name="columns",
        compiler_params=PARAMS,
    )(*near(received, h_high, h_low))

    received = lax.all_to_all(
        message.reshape(ROWS, 8, 128), "row", 0, 0, tiled=True
    ).reshape(256, 128)

    base = pl.pallas_call(
        base_kernel, out_shape=f32(64, 512), in_specs=[VMEM] * 2, out_specs=VMEM, name="base",
        compiler_params=PARAMS,
    )(density.reshape(64, 512), *near(total))
    out = pl.pallas_call(
        finish_kernel,
        out_shape=jax.ShapeDtypeStruct((64, 512), jnp.float32),
        in_specs=[VMEM] * 2,
        out_specs=VMEM,
        name="finish",
        compiler_params=PARAMS,
    )(*near(base, received))
    return out.reshape(2, 2, 16, 512)


def solution(mesh):
    in_specs = (P(None, "hier", "row", None), P("row", None), P(), P(), P(), P(), P())
    out_specs = P(None, "hier", "row", None)
    return jax.shard_map(
        on_device, mesh=mesh, in_specs=in_specs, out_specs=out_specs, check_vma=False
    )
```

```python
import jax
import jax.numpy as jnp
from jax import lax
from jax.experimental import pallas as pl
from jax.experimental.pallas import tpu as pltpu
from jax.sharding import PartitionSpec as P

time_step = 0.25
A1 = time_step
A2 = A1 * time_step / 2
A3 = A2 * time_step / 3

PLANES = 8
ROWS = 32
EDGES = 264


VMEM = pl.BlockSpec(memory_space=pltpu.VMEM)
ANY = pl.BlockSpec(memory_space=pl.ANY)
HBM = pl.BlockSpec(memory_space=pltpu.HBM)
SMEM = pl.BlockSpec(memory_space=pltpu.SMEM)
PARAMS = pltpu.CompilerParams(vmem_limit_bytes=24 << 20)


def f32(*shape):
    return pltpu.VMEM(shape, jnp.float32)


def near(*arrays):
    return [pltpu.with_memory_space_constraint(array, pltpu.VMEM) for array in arrays]


def far(*arrays):
    return [pltpu.with_memory_space_constraint(array, pltpu.HBM) for array in arrays]


def my_plane():
    return lax.axis_index("hier").astype(jnp.int32)


def split_kernel(density, hamiltonian, copies, near_blocks, far_blocks, *scratch):
    rows, own, block, tiles, sems = scratch
    plane = my_plane()
    group = lax.axis_index("row").astype(jnp.int32)
    fetch = pltpu.make_async_copy(density, rows, sems.at[ROWS])
    fetch_own = pltpu.make_async_copy(hamiltonian, own, sems.at[ROWS + 1])
    fetch_own.start()
    fetch.start()
    fetch_own.wait()
    turned = pltpu.roll(own[...], (512 - 16 * group) & 511, 1)
    lane = lax.broadcasted_iota(jnp.int32, (16, 128), 1)
    block[:16] = jnp.where(lane < 16, 0.5 * turned[:, :128], turned[:, :128])
    block[16:32] = turned[:, 128:256]
    last = 0.5 * turned[:, 256:384]
    lane = lax.broadcasted_iota(jnp.int32, (8, 128), 1)
    block[32:] = jnp.where(lane < 16, last[:8], pltpu.roll(last[8:], 16, 1))
    sends = [pltpu.make_async_copy(block, copies.at[r], sems.at[r]) for r in range(ROWS)]
    for send in sends:
        send.start()
    fetch.wait()
    for p in range(4):
        for j in range(4):
            tiles[pl.ds(64 * p + 16 * j, 16), :] = rows[p, :, 128 * j : 128 * j + 128]
    for s in range(PLANES):
        first = 2 * (plane ^ s)
        target = far_blocks if s & 4 else near_blocks
        for a in range(2):
            picked = tiles[pl.ds(first + a, 16, stride=16), :]
            for p in range(4):
                target[s & 3, 8 * p + 4 * a : 8 * p + 4 * a + 4, :] = picked[4 * p : 4 * p + 4]
    for send in sends:
        send.wait()


def join_symmetric(blocks, upper):
    lane = lax.broadcasted_iota(jnp.int32, (8, 128), 1)
    for r in range(ROWS):
        tile, offset = r // 8, 16 * (r % 8)
        for half in range(2):
            at = 8 * half
            first = blocks[r, at : at + 8, :]
            second = blocks[r, 16 + at : 24 + at, :]
            last = blocks[r, 32:40, :]
            if offset:
                first = pltpu.roll(first, offset, 1)
                second = pltpu.roll(second, offset, 1)
            if (offset - 16 * half) % 128:
                last = pltpu.roll(last, (offset - 16 * half) % 128, 1)
            last = jnp.where((lane >= offset) & (lane < offset + 16), last, 0.0)
            if offset:
                parts = [
                    jnp.where(lane >= offset, first, 0.0),
                    jnp.where(lane < offset, first, second),
                    jnp.where(lane < offset, second, last),
                ]
            else:
                parts = [first, second, last]
            parts.append(jnp.zeros_like(first))
            for i in range(4):
                col = 128 * ((tile + i) % 4)
                upper[16 * r + at : 16 * r + at + 8, col : col + 128] = parts[i]
    value = upper[...]
    return value + jnp.transpose(value)


def pack_kernel(near_blocks, far_blocks, *out):
    for s in range(1, 4):
        out[s - 1][0] = near_blocks[s]
        out[s - 1][1] = far_blocks[s]


def prepare_kernel(levels, neighbours, decay, bath, couplings, ints, floats, fields, codes):
    plane = my_plane()
    row = 16 * lax.axis_index("row").astype(jnp.int32) + 2 * plane

    def place(g):
        return (plane ^ (g >> 1)) * 4 + (g & 1)

    count = 0
    for m in range(16):
        for k in range(8):
            lower = neighbours[1, k, m]
            codes[count] = lower * 128 + (8 * m + k)
            count = count + (lower >= 0).astype(jnp.int32)
    ints[3, 0] = count

    def unpack(e, carry):
        code = codes[e]
        m = (code >> 3) & 15
        k = code & 7
        level = levels[k, m].astype(jnp.float32)
        ints[0, e] = place(m)
        ints[1, e] = place(code >> 7)
        ints[2, e] = 8 * k
        floats[0, e] = level * bath[1, k]
        floats[1, e] = level * bath[0, k]
        return carry

    lax.fori_loop(0, count, unpack, 0)
    for m in range(16):
        total = levels[0, m].astype(jnp.float32) * decay[0]
        for k in range(1, 8):
            total = total + levels[k, m].astype(jnp.float32) * decay[k]
        floats[2, place(m)] = total

    values = couplings[...]
    lane = lax.broadcasted_iota(jnp.int32, values.shape, 1)
    for a in range(2):
        own = jnp.sum(jnp.where(lane == row + a, values, 0.0), axis=1, keepdims=True)
        own = jnp.broadcast_to(own, (8, 128))
        for j in range(4):
            here = pl.ds(4 * a + j, 8, stride=8)
            there = values[:, 128 * j : 128 * j + 128]
            fields[0, here, :] = own - there
            fields[1, here, :] = own + there
            fields[2, here, :] = there


def mix(ints, floats, fields, source, both, right):
    def step(e, carry):
        m = ints[0, e]
        q = ints[1, e]
        k = pl.multiple_of(ints[2, e], 8)
        even = floats[0, e]
        odd = floats[1, e]
        xm, ym = source[m], source[m + 2]
        xq, yq = source[q], source[q + 2]
        if both is not None:
            d = fields[0, pl.ds(k, 8), :]
            f = odd * d
            g = even * fields[1, pl.ds(k, 8), :]
            both[m] = both[m] + (g * xq + f * yq)
            both[m + 2] = both[m + 2] + (g * yq - f * xq)
            both[q] = both[q] + d * ym
            both[q + 2] = both[q + 2] - d * xm
        if right is not None:
            c = fields[2, pl.ds(k, 8), :]
            g = even * c
            f = odd * c
            right[m] = right[m] + (g * xq - f * yq)
            right[m + 2] = right[m + 2] + (g * yq + f * xq)
            right[q] = right[q] - c * ym
            right[q + 2] = right[q + 2] + c * xm
        return carry

    lax.fori_loop(0, ints[3, 0], step, 0)


def decayed(floats, source):
    parts = []
    for s in range(PLANES):
        for part in range(2):
            for m in range(2):
                parts.append((-floats[2, 4 * s + m]) * source[4 * s + 2 * part + m])
    return jnp.stack(parts)


def early_kernel(ints_far, floats_far, fields, near_blocks, far_blocks, *refs):
    *pairs, state, first, right, second, ints, floats, sems = refs
    fetches = [
        pltpu.make_async_copy(ints_far, ints, sems.at[0]),
        pltpu.make_async_copy(floats_far, floats, sems.at[1]),
    ]
    for fetch in fetches:
        fetch.start()
    state[0:4] = near_blocks[0].reshape(4, 8, 128)
    state[16:20] = far_blocks[0].reshape(4, 8, 128)
    for s in range(1, 4):
        state[4 * s : 4 * s + 4] = pairs[s - 1][0].reshape(4, 8, 128)
        state[4 * s + 16 : 4 * s + 20] = pairs[s - 1][1].reshape(4, 8, 128)
    right[...] = jnp.zeros_like(right)
    for fetch in fetches:
        fetch.wait()
    first[...] = decayed(floats, state)
    mix(ints, floats, fields, state, first, right)
    first[...] = A2 * state[...] + A3 * first[...]
    second[...] = decayed(floats, first)
    mix(ints, floats, fields, first, second, None)


def gather_rows(ref):
    return jnp.concatenate(
        [
            jnp.concatenate([ref[pl.ds(4 * a + j, 32, stride=8), :] for j in range(4)], axis=1)
            for a in range(2)
        ],
        axis=0,
    )


def spread_rows(ref, value):
    for a in range(2):
        for j in range(4):
            ref[pl.ds(4 * a + j, 32, stride=8), :] = value[
                32 * a : 32 * a + 32, 128 * j : 128 * j + 128
            ]


def halves(value):
    high = value.astype(jnp.bfloat16)
    low = (value - high.astype(jnp.float32)).astype(jnp.bfloat16)
    return high, low


def times_i(value):
    value = value.reshape(PLANES, 2, 2, 8, 128)
    return jnp.concatenate([-value[:, 1:], value[:, :1]], axis=1).reshape(32, 8, 128)


def swap_blocks(value):
    lead = value.shape[0]
    block = lax.broadcasted_iota(jnp.int32, (8, 128), 1) // 16
    for k in range(3):
        width = 16 << k
        low = ((block >> k) & 1) == 0
        pairs = value.reshape(lead, 4 >> k, 2, 1 << k, 8, 128)
        zero, one = pairs[:, :, 0], pairs[:, :, 1]
        shape = zero.shape
        zero = zero.reshape(-1, 128)
        one = one.reshape(-1, 128)
        up = pltpu.roll(one, width, 1)
        down = pltpu.roll(zero, 128 - width, 1)
        low = jnp.broadcast_to(low[None], (zero.shape[0] // 8, 8, 128)).reshape(-1, 128)
        new_zero = jnp.where(low, zero, up).reshape(shape)
        new_one = jnp.where(low, down, one).reshape(shape)
        value = jnp.stack([new_zero, new_one], axis=2).reshape(lead, 8, 8, 128)
    return value


def rows_kernel(ints_far, floats_far, fields, h, state, right, first, second, *refs):
    message, h_high, h_low, ints, floats, rows, p, ep, bp, upper, sems = refs
    plane = my_plane()
    fetches = [
        pltpu.make_async_copy(ints_far, ints, sems.at[0]),
        pltpu.make_async_copy(floats_far, floats, sems.at[1]),
    ]
    for fetch in fetches:
        fetch.start()
    high, low = halves(join_symmetric(h, upper))
    h_high[...] = high
    h_low[...] = low

    def product(value):
        count = value.shape[0]
        value_high, value_low = halves(value)
        main = jnp.dot(
            jnp.concatenate([value_high, value_low], axis=0),
            high,
            preferred_element_type=jnp.float32,
        )
        rest = jnp.dot(value_high, low, preferred_element_type=jnp.float32)
        return main[:count] + main[count:] + rest

    def apply(values):
        stacked = []
        for value in values:
            rows[...] = value.reshape(256, 128)
            stacked.append(gather_rows(rows))
        result = product(jnp.concatenate(stacked, axis=0))
        out = []
        for i in range(len(values)):
            spread_rows(rows, result[64 * i : 64 * i + 64])
            out.append(times_i(rows[...].reshape(32, 8, 128)))
        return out

    s_value = state[...]
    (p_value,) = apply([s_value])
    p[...] = p_value
    v1, edge = apply([first[...] + A3 * p_value, p_value + right[...]])
    for fetch in fetches:
        fetch.wait()
    damped = decayed(floats, p)
    ep[...] = damped
    bp[...] = damped + edge
    mix(ints, floats, fields, p, ep, bp)
    k_value = A2 * p_value + 3 * A3 * bp[...]
    z_value = 0.5 * A1 * s_value + v1 + A3 * ep[...] + 0.5 * second[...]
    v2 = z_value + 0.5 * A1 * s_value + 0.5 * second[...]
    (g_value,) = apply([v2])
    p[...] = z_value
    ep[...] = g_value + decayed(floats, p)
    mix(ints, floats, fields, p, ep, None)
    both = jnp.concatenate(
        [k_value.reshape(8, 4, 8, 128), ep[...].reshape(8, 4, 8, 128)], axis=1
    )
    both = swap_blocks(both)
    for s in range(PLANES):
        start = 2 * (plane ^ s)
        for b in range(8):
            for a in range(2):
                message[pl.ds(start + 16 * b + a, 4, stride=128), :] = both[
                    s, b, 4 * a : 4 * a + 4, :
                ]


def columns_kernel(received, h_high, h_low, message, total):
    value = received[...]
    high, low = halves(value)
    main = jnp.dot(
        h_high[...], jnp.concatenate([high, low], axis=1), preferred_element_type=jnp.float32
    )
    rest = jnp.dot(h_low[...], high, preferred_element_type=jnp.float32)
    z = main[:, :128] + main[:, 128:] + rest
    lane = lax.broadcasted_iota(jnp.int32, z.shape, 1)
    other = pltpu.roll(value, 64, 1)
    result = jnp.where(
        lane < 32, pltpu.roll(z, 96, 1) + other, pltpu.roll(z, 32, 1) - other
    )
    total[...] = result
    tiles = result.reshape(32, 2, 8, 128)
    upper = pltpu.roll(tiles[:, 1].reshape(256, 128), 64, 1)
    lane = lax.broadcasted_iota(jnp.int32, upper.shape, 1)
    message[...] = jnp.where(lane < 64, tiles[:, 0].reshape(256, 128), upper)


def base_kernel(density, total, base):
    base[...] = density[...] + jnp.transpose(total[...])[:64]


def finish_kernel(base, received, out):
    value = swap_blocks(received[...].reshape(4, 8, 8, 128))
    for g in range(4):
        for half in range(2):
            for p in range(4):
                row = slice(16 * p + 8 * half, 16 * p + 8 * half + 8)
                col = slice(128 * g, 128 * g + 128)
                part = value[g, 4 * half + p]
                out[row, col] = base[row, col] + part if p < 2 else base[row, col] - part


def on_device(density, hamiltonian, couplings, decay_rates, bath_coeffs, levels, neighbours):
    copies, near_blocks, far_blocks = pl.pallas_call(
        split_kernel,
        out_shape=[
            pltpu.HBM((ROWS, 40, 128), jnp.float32),
            f32(4, 32, 128),
            f32(4, 32, 128),
        ],
        in_specs=[HBM] * 2,
        out_specs=[HBM] + [VMEM] * 2,
        scratch_shapes=[
            pltpu.VMEM((4, 16, 512), jnp.float32),
            pltpu.VMEM((16, 512), jnp.float32),
            pltpu.VMEM((40, 128), jnp.float32),
            pltpu.VMEM((256, 128), jnp.float32),
            pltpu.SemaphoreType.DMA((ROWS + 2,)),
        ],
        name="split",
        compiler_params=PARAMS,
    )(*far(density.reshape(4, 16, 512), hamiltonian))
    blocks = lax.all_to_all(copies, "row", 0, 0, tiled=True)

    def swap(block, s):
        return lax.ppermute(block, "hier", [(i, i ^ s) for i in range(PLANES)])

    far_blocks = swap(far_blocks, 4)
    packed = pl.pallas_call(
        pack_kernel,
        out_shape=[f32(2, 32, 128)] * 3,
        in_specs=[VMEM] * 2,
        out_specs=[VMEM] * 3,
        name="pack",
        compiler_params=PARAMS,
    )(*near(near_blocks, far_blocks))
    pairs = [swap(packed[s - 1], s) for s in (1, 2, 3)]

    bf16 = pltpu.VMEM((512, 512), jnp.bfloat16)
    whole = pltpu.VMEM((32, 8, 128), jnp.float32)
    ints, floats, fields = pl.pallas_call(
        prepare_kernel,
        out_shape=[
            jax.ShapeDtypeStruct((4, EDGES), jnp.int32),
            jax.ShapeDtypeStruct((3, EDGES), jnp.float32),
            f32(3, 64, 128),
        ],
        in_specs=[SMEM] * 4 + [VMEM],
        out_specs=[SMEM] * 2 + [VMEM],
        scratch_shapes=[pltpu.SMEM((EDGES,), jnp.int32)],
        name="prepare",
        compiler_params=PARAMS,
    )(levels.T, jnp.swapaxes(neighbours, 1, 2), decay_rates, bath_coeffs, couplings)

    state, first, right, second = pl.pallas_call(
        early_kernel,
        out_shape=[whole] * 4,
        in_specs=[ANY] * 2 + [VMEM] * 6,
        out_specs=[VMEM] * 4,
        scratch_shapes=[
            pltpu.SMEM((4, EDGES), jnp.int32),
            pltpu.SMEM((3, EDGES), jnp.float32),
            pltpu.SemaphoreType.DMA((2,)),
        ],
        name="early",
        compiler_params=PARAMS,
    )(ints, floats, *near(fields, near_blocks, far_blocks, *pairs))

    message, h_high, h_low = pl.pallas_call(
        rows_kernel,
        out_shape=[f32(512, 128), bf16, bf16],
        in_specs=[ANY] * 2 + [VMEM] * 6,
        out_specs=[VMEM] * 3,
        scratch_shapes=[
            pltpu.SMEM((4, EDGES), jnp.int32),
            pltpu.SMEM((3, EDGES), jnp.float32),
            pltpu.VMEM((256, 128), jnp.float32),
            *[whole] * 3,
            pltpu.VMEM((512, 512), jnp.float32),
            pltpu.SemaphoreType.DMA((2,)),
        ],
        name="rows",
        compiler_params=PARAMS,
    )(ints, floats, *near(fields, blocks, state, right, first, second))

    received = lax.all_to_all(
        message.reshape(256, 2, 128), ("row", "hier"), 0, 0, tiled=True
    ).reshape(512, 128)

    message, total = pl.pallas_call(
        columns_kernel,
        out_shape=[f32(256, 128), f32(512, 128)],
        in_specs=[VMEM] * 3,
        out_specs=[VMEM] * 2,
        name="columns",
        compiler_params=PARAMS,
    )(*near(received, h_high, h_low))

    received = lax.all_to_all(
        message.reshape(ROWS, 8, 128), "row", 0, 0, tiled=True
    ).reshape(256, 128)

    base = pl.pallas_call(
        base_kernel, out_shape=f32(64, 512), in_specs=[VMEM] * 2, out_specs=VMEM, name="base",
        compiler_params=PARAMS,
    )(density.reshape(64, 512), *near(total))
    out = pl.pallas_call(
        finish_kernel,
        out_shape=jax.ShapeDtypeStruct((64, 512), jnp.float32),
        in_specs=[VMEM] * 2,
        out_specs=VMEM,
        name="finish",
        compiler_params=PARAMS,
    )(*near(base, received))
    return out.reshape(2, 2, 16, 512)


def solution(mesh):
    in_specs = (P(None, "hier", "row", None), P("row", None), P(), P(), P(), P(), P())
    out_specs = P(None, "hier", "row", None)
    return jax.shard_map(
        on_device, mesh=mesh, in_specs=in_specs, out_specs=out_specs, check_vma=False
    )
```

```python
import jax
import jax.numpy as jnp
from jax import lax
from jax.experimental import pallas as pl
from jax.experimental.pallas import tpu as pltpu
from jax.sharding import PartitionSpec as P

time_step = 0.25
A1 = time_step
A2 = A1 * time_step / 2
A3 = A2 * time_step / 3

PLANES = 8
CHIPS = 16
SAME_CORE = [list(range(core, 2 * CHIPS, 2)) for core in range(2)]
EDGES = 264


VMEM = pl.BlockSpec(memory_space=pltpu.VMEM)
ANY = pl.BlockSpec(memory_space=pl.ANY)
HBM = pl.BlockSpec(memory_space=pltpu.HBM)
SMEM = pl.BlockSpec(memory_space=pltpu.SMEM)
PARAMS = pltpu.CompilerParams(vmem_limit_bytes=24 << 20)


def f32(*shape):
    return pltpu.VMEM(shape, jnp.float32)


def near(*arrays):
    return [pltpu.with_memory_space_constraint(array, pltpu.VMEM) for array in arrays]


def far(*arrays):
    return [pltpu.with_memory_space_constraint(array, pltpu.HBM) for array in arrays]


def my_plane():
    return lax.axis_index("hier").astype(jnp.int32)


def split_kernel(density, hamiltonian, *refs):
    tables, (copies, near_blocks, far_blocks), held = refs[:5], refs[5:8], refs[8:13]
    rows, own, block, tiles, sems = refs[13:]
    plane = my_plane()
    group = lax.axis_index("row").astype(jnp.int32)
    fetch = pltpu.make_async_copy(density, rows, sems.at[CHIPS])
    fetch_own = pltpu.make_async_copy(hamiltonian, own, sems.at[CHIPS + 1])
    fetch_own.start()
    fetch.start()
    loads = [
        pltpu.make_async_copy(table, place, sems.at[CHIPS + 2 + i])
        for i, (table, place) in enumerate(zip(tables, held))
    ]
    for load in loads:
        load.start()
    fetch_own.wait()
    turned = pltpu.roll(own[...], (512 - 16 * group) & 511, 1)
    lane = lax.broadcasted_iota(jnp.int32, (16, 128), 1)
    block[:16] = jnp.where(lane < 16, 0.5 * turned[:, :128], turned[:, :128])
    block[16:32] = turned[:, 128:256]
    last = 0.5 * turned[:, 256:384]
    lane = lax.broadcasted_iota(jnp.int32, (8, 128), 1)
    block[32:] = jnp.where(lane < 16, last[:8], pltpu.roll(last[8:], 16, 1))
    sends = [pltpu.make_async_copy(block, copies.at[r], sems.at[r]) for r in range(CHIPS)]
    for send in sends:
        send.start()
    fetch.wait()
    for p in range(4):
        for j in range(4):
            tiles[pl.ds(64 * p + 16 * j, 16), :] = rows[p, :, 128 * j : 128 * j + 128]
    for s in range(PLANES):
        first = 2 * (plane ^ s)
        target = far_blocks if s & 4 else near_blocks
        for a in range(2):
            picked = tiles[pl.ds(first + a, 16, stride=16), :]
            for p in range(4):
                target[s & 3, 8 * p + 4 * a : 8 * p + 4 * a + 4, :] = picked[4 * p : 4 * p + 4]
    for wait in sends + loads:
        wait.wait()


def join_symmetric(mine, other, upper):
    lane = lax.broadcasted_iota(jnp.int32, (8, 128), 1)
    even = (lax.axis_index("row") & 1) == 0
    for r in range(2 * CHIPS):
        tile, offset = r // 8, 16 * (r % 8)

        def part(at):
            pair = (mine[r // 2, at : at + 8, :], other[r // 2, at : at + 8, :])
            return jnp.where(even, pair[r % 2], pair[1 - r % 2])

        for half in range(2):
            at = 8 * half
            first = part(at)
            second = part(16 + at)
            last = part(32)
            if offset:
                first = pltpu.roll(first, offset, 1)
                second = pltpu.roll(second, offset, 1)
            if (offset - 16 * half) % 128:
                last = pltpu.roll(last, (offset - 16 * half) % 128, 1)
            last = jnp.where((lane >= offset) & (lane < offset + 16), last, 0.0)
            if offset:
                parts = [
                    jnp.where(lane >= offset, first, 0.0),
                    jnp.where(lane < offset, first, second),
                    jnp.where(lane < offset, second, last),
                ]
            else:
                parts = [first, second, last]
            parts.append(jnp.zeros_like(first))
            for i in range(4):
                col = 128 * ((tile + i) % 4)
                upper[16 * r + at : 16 * r + at + 8, col : col + 128] = parts[i]
    value = upper[...]
    return value + jnp.transpose(value)


def sites_kernel(mine, other, h_high, h_low, upper):
    high, low = halves(join_symmetric(mine, other, upper))
    h_high[...] = high
    h_low[...] = low


def pack_kernel(near_blocks, far_blocks, *out):
    for s in range(1, 4):
        out[s - 1][0] = near_blocks[s]
        out[s - 1][1] = far_blocks[s]


def prepare_kernel(levels, neighbours, decay, bath, couplings, ints, floats, fields, codes):
    plane = my_plane()
    row = 16 * lax.axis_index("row").astype(jnp.int32) + 2 * plane

    def place(g):
        return (plane ^ (g >> 1)) * 4 + (g & 1)

    count = 0
    for m in range(16):
        for k in range(8):
            lower = neighbours[1, k, m]
            codes[count] = lower * 128 + (8 * m + k)
            count = count + (lower >= 0).astype(jnp.int32)
    ints[3, 0] = count

    def unpack(e, carry):
        code = codes[e]
        m = (code >> 3) & 15
        k = code & 7
        level = levels[k, m].astype(jnp.float32)
        ints[0, e] = place(m)
        ints[1, e] = place(code >> 7)
        ints[2, e] = 8 * k
        floats[0, e] = level * bath[1, k]
        floats[1, e] = level * bath[0, k]
        return carry

    lax.fori_loop(0, count, unpack, 0)
    for m in range(16):
        total = levels[0, m].astype(jnp.float32) * decay[0]
        for k in range(1, 8):
            total = total + levels[k, m].astype(jnp.float32) * decay[k]
        floats[2, place(m)] = total

    values = couplings[...]
    lane = lax.broadcasted_iota(jnp.int32, values.shape, 1)
    for a in range(2):
        own = jnp.sum(jnp.where(lane == row + a, values, 0.0), axis=1, keepdims=True)
        own = jnp.broadcast_to(own, (8, 128))
        for j in range(4):
            here = pl.ds(4 * a + j, 8, stride=8)
            there = values[:, 128 * j : 128 * j + 128]
            fields[0, here, :] = own - there
            fields[1, here, :] = own + there
            fields[2, here, :] = there


def mix(ints, floats, fields, source, both, right):
    def step(e, carry):
        m = ints[0, e]
        q = ints[1, e]
        k = pl.multiple_of(ints[2, e], 8)
        even = floats[0, e]
        odd = floats[1, e]
        xm, ym = source[m], source[m + 2]
        xq, yq = source[q], source[q + 2]
        if both is not None:
            d = fields[0, pl.ds(k, 8), :]
            f = odd * d
            g = even * fields[1, pl.ds(k, 8), :]
            both[m] = both[m] + (g * xq + f * yq)
            both[m + 2] = both[m + 2] + (g * yq - f * xq)
            both[q] = both[q] + d * ym
            both[q + 2] = both[q + 2] - d * xm
        if right is not None:
            c = fields[2, pl.ds(k, 8), :]
            g = even * c
            f = odd * c
            right[m] = right[m] + (g * xq - f * yq)
            right[m + 2] = right[m + 2] + (g * yq + f * xq)
            right[q] = right[q] - c * ym
            right[q + 2] = right[q + 2] + c * xm
        return carry

    lax.fori_loop(0, ints[3, 0], step, 0)


def decayed(floats, source):
    parts = []
    for s in range(PLANES):
        for part in range(2):
            for m in range(2):
                parts.append((-floats[2, 4 * s + m]) * source[4 * s + 2 * part + m])
    return jnp.stack(parts)


def gather_rows(ref):
    return jnp.concatenate(
        [
            jnp.concatenate([ref[pl.ds(4 * a + j, 32, stride=8), :] for j in range(4)], axis=1)
            for a in range(2)
        ],
        axis=0,
    )


def spread_rows(ref, value):
    for a in range(2):
        for j in range(4):
            ref[pl.ds(4 * a + j, 32, stride=8), :] = value[
                32 * a : 32 * a + 32, 128 * j : 128 * j + 128
            ]


def halves(value):
    high = value.astype(jnp.bfloat16)
    low = (value - high.astype(jnp.float32)).astype(jnp.bfloat16)
    return high, low


def times_i(value):
    value = value.reshape(PLANES, 2, 2, 8, 128)
    return jnp.concatenate([-value[:, 1:], value[:, :1]], axis=1).reshape(32, 8, 128)


def swap_blocks(value):
    lead = value.shape[0]
    block = lax.broadcasted_iota(jnp.int32, (8, 128), 1) // 16
    for k in range(3):
        width = 16 << k
        low = ((block >> k) & 1) == 0
        pairs = value.reshape(lead, 4 >> k, 2, 1 << k, 8, 128)
        zero, one = pairs[:, :, 0], pairs[:, :, 1]
        shape = zero.shape
        zero = zero.reshape(-1, 128)
        one = one.reshape(-1, 128)
        up = pltpu.roll(one, width, 1)
        down = pltpu.roll(zero, 128 - width, 1)
        low = jnp.broadcast_to(low[None], (zero.shape[0] // 8, 8, 128)).reshape(-1, 128)
        new_zero = jnp.where(low, zero, up).reshape(shape)
        new_one = jnp.where(low, down, one).reshape(shape)
        value = jnp.stack([new_zero, new_one], axis=2).reshape(lead, 8, 8, 128)
    return value


def rows_kernel(ints_far, floats_far, fields, h_high, h_low, near_blocks, far_blocks, *refs):
    *pairs, message, ints, floats, rows, state, first, right, second, p, ep, bp, sems = refs
    plane = my_plane()
    fetches = [
        pltpu.make_async_copy(ints_far, ints, sems.at[0]),
        pltpu.make_async_copy(floats_far, floats, sems.at[1]),
    ]
    for fetch in fetches:
        fetch.start()
    state[0:4] = near_blocks[0].reshape(4, 8, 128)
    state[16:20] = far_blocks[0].reshape(4, 8, 128)
    for s in range(1, 4):
        state[4 * s : 4 * s + 4] = pairs[s - 1][0].reshape(4, 8, 128)
        state[4 * s + 16 : 4 * s + 20] = pairs[s - 1][1].reshape(4, 8, 128)
    right[...] = jnp.zeros_like(right)
    high, low = h_high[...], h_low[...]

    def product(value):
        count = value.shape[0]
        value_high, value_low = halves(value)
        main = jnp.dot(
            jnp.concatenate([value_high, value_low], axis=0),
            high,
            preferred_element_type=jnp.float32,
        )
        rest = jnp.dot(value_high, low, preferred_element_type=jnp.float32)
        return main[:count] + main[count:] + rest

    def apply(values):
        stacked = []
        for value in values:
            rows[...] = value.reshape(256, 128)
            stacked.append(gather_rows(rows))
        result = product(jnp.concatenate(stacked, axis=0))
        out = []
        for i in range(len(values)):
            spread_rows(rows, result[64 * i : 64 * i + 64])
            out.append(times_i(rows[...].reshape(32, 8, 128)))
        return out

    s_value = state[...]
    (p_value,) = apply([s_value])
    p[...] = p_value
    for fetch in fetches:
        fetch.wait()
    first[...] = decayed(floats, state)
    mix(ints, floats, fields, state, first, right)
    first[...] = A2 * state[...] + A3 * first[...]
    second[...] = decayed(floats, first)
    mix(ints, floats, fields, first, second, None)
    v1, edge = apply([first[...] + A3 * p_value, p_value + right[...]])
    damped = decayed(floats, p)
    ep[...] = damped
    bp[...] = damped + edge
    mix(ints, floats, fields, p, ep, bp)
    k_value = A2 * p_value + 3 * A3 * bp[...]
    z_value = 0.5 * A1 * s_value + v1 + A3 * ep[...] + 0.5 * second[...]
    v2 = z_value + 0.5 * A1 * s_value + 0.5 * second[...]
    (g_value,) = apply([v2])
    p[...] = z_value
    ep[...] = g_value + decayed(floats, p)
    mix(ints, floats, fields, p, ep, None)
    both = jnp.concatenate(
        [k_value.reshape(8, 4, 8, 128), ep[...].reshape(8, 4, 8, 128)], axis=1
    )
    both = swap_blocks(both)
    for s in range(PLANES):
        start = 2 * (plane ^ s)
        for b in range(8):
            for a in range(2):
                message[pl.ds(start + 16 * b + a, 4, stride=128), :] = both[
                    s, b, 4 * a : 4 * a + 4, :
                ]


def columns_kernel(received, h_high, h_low, message, total):
    value = received[...]
    high, low = halves(value)
    main = jnp.dot(
        h_high[...], jnp.concatenate([high, low], axis=1), preferred_element_type=jnp.float32
    )
    rest = jnp.dot(h_low[...], high, preferred_element_type=jnp.float32)
    z = main[:, :128] + main[:, 128:] + rest
    lane = lax.broadcasted_iota(jnp.int32, z.shape, 1)
    other = pltpu.roll(value, 64, 1)
    result = jnp.where(
        lane < 32, pltpu.roll(z, 96, 1) + other, pltpu.roll(z, 32, 1) - other
    )
    total[...] = result
    tiles = result.reshape(32, 2, 8, 128)
    upper = pltpu.roll(tiles[:, 1].reshape(256, 128), 64, 1)
    lane = lax.broadcasted_iota(jnp.int32, upper.shape, 1)
    message[...] = jnp.where(lane < 64, tiles[:, 0].reshape(256, 128), upper)


def base_kernel(density, total, base):
    base[...] = density[...] + jnp.transpose(total[...])[:64]


def finish_kernel(base, received, out):
    value = swap_blocks(received[...].reshape(4, 8, 8, 128))
    for g in range(4):
        for half in range(2):
            for p in range(4):
                row = slice(16 * p + 8 * half, 16 * p + 8 * half + 8)
                col = slice(128 * g, 128 * g + 128)
                part = value[g, 4 * half + p]
                out[row, col] = base[row, col] + part if p < 2 else base[row, col] - part


def on_device(density, hamiltonian, couplings, decay_rates, bath_coeffs, levels, neighbours):
    tables = (levels.T, jnp.swapaxes(neighbours, 1, 2), decay_rates, bath_coeffs, couplings)
    copies, near_blocks, far_blocks, *tables = pl.pallas_call(
        split_kernel,
        out_shape=[
            pltpu.HBM((CHIPS, 40, 128), jnp.float32),
            f32(4, 32, 128),
            f32(4, 32, 128),
            *[pltpu.VMEM(table.shape, table.dtype) for table in tables],
        ],
        in_specs=[HBM] * 7,
        out_specs=[HBM] + [VMEM] * 7,
        scratch_shapes=[
            pltpu.VMEM((4, 16, 512), jnp.float32),
            pltpu.VMEM((16, 512), jnp.float32),
            pltpu.VMEM((40, 128), jnp.float32),
            pltpu.VMEM((256, 128), jnp.float32),
            pltpu.SemaphoreType.DMA((CHIPS + 7,)),
        ],
        name="split",
        compiler_params=PARAMS,
    )(*far(density.reshape(4, 16, 512), hamiltonian, *tables))
    mine = lax.all_to_all(copies, "row", 0, 0, axis_index_groups=SAME_CORE, tiled=True)
    other = lax.ppermute(mine, "row", [(i, i ^ 1) for i in range(2 * CHIPS)])

    def swap(block, s):
        return lax.ppermute(block, "hier", [(i, i ^ s) for i in range(PLANES)])

    far_blocks = swap(far_blocks, 4)
    packed = pl.pallas_call(
        pack_kernel,
        out_shape=[f32(2, 32, 128)] * 3,
        in_specs=[VMEM] * 2,
        out_specs=[VMEM] * 3,
        name="pack",
        compiler_params=PARAMS,
    )(*near(near_blocks, far_blocks))
    pairs = [swap(packed[s - 1], s) for s in (3, 2, 1)][::-1]

    bf16 = pltpu.VMEM((512, 512), jnp.bfloat16)
    whole = pltpu.VMEM((32, 8, 128), jnp.float32)
    ints, floats, fields = pl.pallas_call(
        prepare_kernel,
        out_shape=[
            jax.ShapeDtypeStruct((4, EDGES), jnp.int32),
            jax.ShapeDtypeStruct((3, EDGES), jnp.float32),
            f32(3, 64, 128),
        ],
        in_specs=[SMEM] * 4 + [VMEM],
        out_specs=[SMEM] * 2 + [VMEM],
        scratch_shapes=[pltpu.SMEM((EDGES,), jnp.int32)],
        name="prepare",
        compiler_params=PARAMS,
    )(*tables[:4], *near(tables[4]))

    h_high, h_low = pl.pallas_call(
        sites_kernel,
        out_shape=[bf16, bf16],
        in_specs=[VMEM] * 2,
        out_specs=[VMEM] * 2,
        scratch_shapes=[pltpu.VMEM((512, 512), jnp.float32)],
        name="sites",
        compiler_params=PARAMS,
    )(*near(mine, other))

    message = pl.pallas_call(
        rows_kernel,
        out_shape=f32(512, 128),
        in_specs=[ANY] * 2 + [VMEM] * 8,
        out_specs=VMEM,
        scratch_shapes=[
            pltpu.SMEM((4, EDGES), jnp.int32),
            pltpu.SMEM((3, EDGES), jnp.float32),
            pltpu.VMEM((256, 128), jnp.float32),
            *[whole] * 7,
            pltpu.SemaphoreType.DMA((2,)),
        ],
        name="rows",
        compiler_params=PARAMS,
    )(ints, floats, *near(fields, h_high, h_low, near_blocks, far_blocks, *pairs))

    received = lax.all_to_all(
        message.reshape(256, 2, 128), ("row", "hier"), 0, 0, tiled=True
    ).reshape(512, 128)

    message, total = pl.pallas_call(
        columns_kernel,
        out_shape=[f32(256, 128), f32(512, 128)],
        in_specs=[VMEM] * 3,
        out_specs=[VMEM] * 2,
        name="columns",
        compiler_params=PARAMS,
    )(*near(received, h_high, h_low))

    received = lax.all_to_all(
        message.reshape(2 * CHIPS, 8, 128), "row", 0, 0, tiled=True
    ).reshape(256, 128)

    base = pl.pallas_call(
        base_kernel, out_shape=f32(64, 512), in_specs=[VMEM] * 2, out_specs=VMEM, name="base",
        compiler_params=PARAMS,
    )(density.reshape(64, 512), *near(total))
    out = pl.pallas_call(
        finish_kernel,
        out_shape=jax.ShapeDtypeStruct((64, 512), jnp.float32),
        in_specs=[VMEM] * 2,
        out_specs=VMEM,
        name="finish",
        compiler_params=PARAMS,
    )(*near(base, received))
    return out.reshape(2, 2, 16, 512)


def solution(mesh):
    in_specs = (P(None, "hier", "row", None), P("row", None), P(), P(), P(), P(), P())
    out_specs = P(None, "hier", "row", None)
    return jax.shard_map(
        on_device, mesh=mesh, in_specs=in_specs, out_specs=out_specs, check_vma=False
    )
```

```python
import jax
import jax.numpy as jnp
from jax import lax
from jax.experimental import pallas as pl
from jax.experimental.pallas import tpu as pltpu
from jax.sharding import PartitionSpec as P

time_step = 0.25
A1 = time_step
A2 = A1 * time_step / 2
A3 = A2 * time_step / 3

PLANES = 8
CHIPS = 16
SAME_CORE = [list(range(core, 2 * CHIPS, 2)) for core in range(2)]
EDGES = 264


VMEM = pl.BlockSpec(memory_space=pltpu.VMEM)
ANY = pl.BlockSpec(memory_space=pl.ANY)
HBM = pl.BlockSpec(memory_space=pltpu.HBM)
SMEM = pl.BlockSpec(memory_space=pltpu.SMEM)
PARAMS = pltpu.CompilerParams(vmem_limit_bytes=24 << 20)


def f32(*shape):
    return pltpu.VMEM(shape, jnp.float32)


def near(*arrays):
    return [pltpu.with_memory_space_constraint(array, pltpu.VMEM) for array in arrays]


def far(*arrays):
    return [pltpu.with_memory_space_constraint(array, pltpu.HBM) for array in arrays]


def my_plane():
    return lax.axis_index("hier").astype(jnp.int32)


def split_kernel(density, hamiltonian, *refs):
    tables, (copies, near_blocks, far_blocks), held = refs[:5], refs[5:8], refs[8:13]
    rows, own, block, tiles, sems = refs[13:]
    plane = my_plane()
    group = lax.axis_index("row").astype(jnp.int32)
    fetch = pltpu.make_async_copy(density, rows, sems.at[CHIPS])
    fetch_own = pltpu.make_async_copy(hamiltonian, own, sems.at[CHIPS + 1])
    fetch_own.start()
    fetch.start()
    loads = [
        pltpu.make_async_copy(table, place, sems.at[CHIPS + 2 + i])
        for i, (table, place) in enumerate(zip(tables, held))
    ]
    for load in loads:
        load.start()
    fetch_own.wait()
    turned = pltpu.roll(own[...], (512 - 16 * group) & 511, 1)
    lane = lax.broadcasted_iota(jnp.int32, (16, 128), 1)
    block[:16] = jnp.where(lane < 16, 0.5 * turned[:, :128], turned[:, :128])
    block[16:32] = turned[:, 128:256]
    last = 0.5 * turned[:, 256:384]
    lane = lax.broadcasted_iota(jnp.int32, (8, 128), 1)
    block[32:] = jnp.where(lane < 16, last[:8], pltpu.roll(last[8:], 16, 1))
    sends = [pltpu.make_async_copy(block, copies.at[r], sems.at[r]) for r in range(CHIPS)]
    for send in sends:
        send.start()
    fetch.wait()
    for p in range(4):
        for j in range(4):
            tiles[pl.ds(64 * p + 16 * j, 16), :] = rows[p, :, 128 * j : 128 * j + 128]
    for s in range(PLANES):
        first = 2 * (plane ^ s)
        target = far_blocks if s & 4 else near_blocks
        for a in range(2):
            picked = tiles[pl.ds(first + a, 16, stride=16), :]
            for p in range(4):
                target[s & 3, 8 * p + 4 * a : 8 * p + 4 * a + 4, :] = picked[4 * p : 4 * p + 4]
    for wait in sends + loads:
        wait.wait()


def join_symmetric(mine, other, upper):
    lane = lax.broadcasted_iota(jnp.int32, (8, 128), 1)
    even = (lax.axis_index("row") & 1) == 0
    for r in range(2 * CHIPS):
        tile, offset = r // 8, 16 * (r % 8)

        def part(at):
            pair = (mine[r // 2, at : at + 8, :], other[r // 2, at : at + 8, :])
            return jnp.where(even, pair[r % 2], pair[1 - r % 2])

        for half in range(2):
            at = 8 * half
            first = part(at)
            second = part(16 + at)
            last = part(32)
            if offset:
                first = pltpu.roll(first, offset, 1)
                second = pltpu.roll(second, offset, 1)
            if (offset - 16 * half) % 128:
                last = pltpu.roll(last, (offset - 16 * half) % 128, 1)
            last = jnp.where((lane >= offset) & (lane < offset + 16), last, 0.0)
            if offset:
                parts = [
                    jnp.where(lane >= offset, first, 0.0),
                    jnp.where(lane < offset, first, second),
                    jnp.where(lane < offset, second, last),
                ]
            else:
                parts = [first, second, last]
            parts.append(jnp.zeros_like(first))
            for i in range(4):
                col = 128 * ((tile + i) % 4)
                upper[16 * r + at : 16 * r + at + 8, col : col + 128] = parts[i]
    value = upper[...]
    return value + jnp.transpose(value)


def sites_kernel(mine, other, h_high, h_low, upper):
    high, low = halves(join_symmetric(mine, other, upper))
    h_high[...] = high
    h_low[...] = low


def pack_kernel(near_blocks, far_blocks, *out):
    for s in range(1, 4):
        out[s - 1][0] = near_blocks[s]
        out[s - 1][1] = far_blocks[s]


def prepare_kernel(levels, neighbours, decay, bath, couplings, ints, floats, fields, codes):
    plane = my_plane()
    row = 16 * lax.axis_index("row").astype(jnp.int32) + 2 * plane

    def place(g):
        return (plane ^ (g >> 1)) * 4 + (g & 1)

    count = 0
    for m in range(16):
        for k in range(8):
            lower = neighbours[1, k, m]
            codes[count] = lower * 128 + (8 * m + k)
            count = count + (lower >= 0).astype(jnp.int32)
    ints[3, 0] = count

    def unpack(e, carry):
        code = codes[e]
        m = (code >> 3) & 15
        k = code & 7
        level = levels[k, m].astype(jnp.float32)
        ints[0, e] = place(m)
        ints[1, e] = place(code >> 7)
        ints[2, e] = 8 * k
        floats[0, e] = level * bath[1, k]
        floats[1, e] = level * bath[0, k]
        return carry

    lax.fori_loop(0, count, unpack, 0)
    for m in range(16):
        total = levels[0, m].astype(jnp.float32) * decay[0]
        for k in range(1, 8):
            total = total + levels[k, m].astype(jnp.float32) * decay[k]
        floats[2, place(m)] = total

    values = couplings[...]
    lane = lax.broadcasted_iota(jnp.int32, values.shape, 1)
    for a in range(2):
        own = jnp.sum(jnp.where(lane == row + a, values, 0.0), axis=1, keepdims=True)
        own = jnp.broadcast_to(own, (8, 128))
        for j in range(4):
            here = pl.ds(4 * a + j, 8, stride=8)
            there = values[:, 128 * j : 128 * j + 128]
            fields[0, here, :] = own - there
            fields[1, here, :] = own + there
            fields[2, here, :] = there


def mix(ints, floats, fields, *jobs):
    def step(e, carry):
        m = ints[0, e]
        q = ints[1, e]
        k = pl.multiple_of(ints[2, e], 8)
        even = floats[0, e]
        odd = floats[1, e]
        d = fields[0, pl.ds(k, 8), :]
        f = odd * d
        g = even * fields[1, pl.ds(k, 8), :]
        for source, both, right in jobs:
            xm, ym = source[m], source[m + 2]
            xq, yq = source[q], source[q + 2]
            both[m] = both[m] + (g * xq + f * yq)
            both[m + 2] = both[m + 2] + (g * yq - f * xq)
            both[q] = both[q] + d * ym
            both[q + 2] = both[q + 2] - d * xm
            if right is not None:
                c = fields[2, pl.ds(k, 8), :]
                gr = even * c
                fr = odd * c
                right[m] = right[m] + (gr * xq - fr * yq)
                right[m + 2] = right[m + 2] + (gr * yq + fr * xq)
                right[q] = right[q] - c * ym
                right[q + 2] = right[q + 2] + c * xm
        return carry

    lax.fori_loop(0, ints[3, 0], step, 0)


def decayed(floats, source):
    parts = []
    for s in range(PLANES):
        for part in range(2):
            for m in range(2):
                parts.append((-floats[2, 4 * s + m]) * source[4 * s + 2 * part + m])
    return jnp.stack(parts)


def gather_rows(ref):
    return jnp.concatenate(
        [
            jnp.concatenate([ref[pl.ds(4 * a + j, 32, stride=8), :] for j in range(4)], axis=1)
            for a in range(2)
        ],
        axis=0,
    )


def spread_rows(ref, value):
    for a in range(2):
        for j in range(4):
            ref[pl.ds(4 * a + j, 32, stride=8), :] = value[
                32 * a : 32 * a + 32, 128 * j : 128 * j + 128
            ]


def halves(value):
    high = value.astype(jnp.bfloat16)
    low = (value - high.astype(jnp.float32)).astype(jnp.bfloat16)
    return high, low


def times_i(value):
    value = value.reshape(PLANES, 2, 2, 8, 128)
    return jnp.concatenate([-value[:, 1:], value[:, :1]], axis=1).reshape(32, 8, 128)


def swap_blocks(value):
    lead = value.shape[0]
    block = lax.broadcasted_iota(jnp.int32, (8, 128), 1) // 16
    for k in range(3):
        width = 16 << k
        low = ((block >> k) & 1) == 0
        pairs = value.reshape(lead, 4 >> k, 2, 1 << k, 8, 128)
        zero, one = pairs[:, :, 0], pairs[:, :, 1]
        shape = zero.shape
        zero = zero.reshape(-1, 128)
        one = one.reshape(-1, 128)
        up = pltpu.roll(one, width, 1)
        down = pltpu.roll(zero, 128 - width, 1)
        low = jnp.broadcast_to(low[None], (zero.shape[0] // 8, 8, 128)).reshape(-1, 128)
        new_zero = jnp.where(low, zero, up).reshape(shape)
        new_one = jnp.where(low, down, one).reshape(shape)
        value = jnp.stack([new_zero, new_one], axis=2).reshape(lead, 8, 8, 128)
    return value


def rows_kernel(ints_far, floats_far, fields, h_high, h_low, near_blocks, far_blocks, *refs):
    *pairs, message, ints, floats, rows, state, first, right, second, p, ep, bp, sems = refs
    plane = my_plane()
    fetches = [
        pltpu.make_async_copy(ints_far, ints, sems.at[0]),
        pltpu.make_async_copy(floats_far, floats, sems.at[1]),
    ]
    for fetch in fetches:
        fetch.start()
    state[0:4] = near_blocks[0].reshape(4, 8, 128)
    state[16:20] = far_blocks[0].reshape(4, 8, 128)
    for s in range(1, 4):
        state[4 * s : 4 * s + 4] = pairs[s - 1][0].reshape(4, 8, 128)
        state[4 * s + 16 : 4 * s + 20] = pairs[s - 1][1].reshape(4, 8, 128)
    right[...] = jnp.zeros_like(right)
    high, low = h_high[...], h_low[...]

    def product(value):
        count = value.shape[0]
        value_high, value_low = halves(value)
        main = jnp.dot(
            jnp.concatenate([value_high, value_low], axis=0),
            high,
            preferred_element_type=jnp.float32,
        )
        rest = jnp.dot(value_high, low, preferred_element_type=jnp.float32)
        return main[:count] + main[count:] + rest

    def apply(values):
        stacked = []
        for value in values:
            rows[...] = value.reshape(256, 128)
            stacked.append(gather_rows(rows))
        result = product(jnp.concatenate(stacked, axis=0))
        out = []
        for i in range(len(values)):
            spread_rows(rows, result[64 * i : 64 * i + 64])
            out.append(times_i(rows[...].reshape(32, 8, 128)))
        return out

    s_value = state[...]
    (p_value,) = apply([s_value])
    p[...] = p_value
    for fetch in fetches:
        fetch.wait()
    first[...] = decayed(floats, state)
    mix(ints, floats, fields, (state, first, right))
    first[...] = A2 * state[...] + A3 * first[...]
    second[...] = decayed(floats, first)
    v1, edge = apply([first[...] + A3 * p_value, p_value + right[...]])
    damped = decayed(floats, p)
    ep[...] = damped
    bp[...] = damped + edge
    mix(ints, floats, fields, (p, ep, bp), (first, second, None))
    k_value = A2 * p_value + 3 * A3 * bp[...]
    z_value = 0.5 * A1 * s_value + v1 + A3 * ep[...] + 0.5 * second[...]
    v2 = z_value + 0.5 * A1 * s_value + 0.5 * second[...]
    (g_value,) = apply([v2])
    p[...] = z_value
    ep[...] = g_value + decayed(floats, p)
    mix(ints, floats, fields, (p, ep, None))
    both = jnp.concatenate(
        [k_value.reshape(8, 4, 8, 128), ep[...].reshape(8, 4, 8, 128)], axis=1
    )
    both = swap_blocks(both)
    for s in range(PLANES):
        start = 2 * (plane ^ s)
        for b in range(8):
            for a in range(2):
                message[pl.ds(start + 16 * b + a, 4, stride=128), :] = both[
                    s, b, 4 * a : 4 * a + 4, :
                ]


def columns_kernel(received, h_high, h_low, message, total):
    value = received[...]
    high, low = halves(value)
    main = jnp.dot(
        h_high[...], jnp.concatenate([high, low], axis=1), preferred_element_type=jnp.float32
    )
    rest = jnp.dot(h_low[...], high, preferred_element_type=jnp.float32)
    z = main[:, :128] + main[:, 128:] + rest
    lane = lax.broadcasted_iota(jnp.int32, z.shape, 1)
    other = pltpu.roll(value, 64, 1)
    result = jnp.where(
        lane < 32, pltpu.roll(z, 96, 1) + other, pltpu.roll(z, 32, 1) - other
    )
    total[...] = result
    tiles = result.reshape(32, 2, 8, 128)
    upper = pltpu.roll(tiles[:, 1].reshape(256, 128), 64, 1)
    lane = lax.broadcasted_iota(jnp.int32, upper.shape, 1)
    message[...] = jnp.where(lane < 64, tiles[:, 0].reshape(256, 128), upper)


def base_kernel(density, total, base):
    base[...] = density[...] + jnp.transpose(total[...])[:64]


def finish_kernel(base, received, out):
    value = swap_blocks(received[...].reshape(4, 8, 8, 128))
    for g in range(4):
        for half in range(2):
            for p in range(4):
                row = slice(16 * p + 8 * half, 16 * p + 8 * half + 8)
                col = slice(128 * g, 128 * g + 128)
                part = value[g, 4 * half + p]
                out[row, col] = base[row, col] + part if p < 2 else base[row, col] - part


def on_device(density, hamiltonian, couplings, decay_rates, bath_coeffs, levels, neighbours):
    tables = (levels.T, jnp.swapaxes(neighbours, 1, 2), decay_rates, bath_coeffs, couplings)
    copies, near_blocks, far_blocks, *tables = pl.pallas_call(
        split_kernel,
        out_shape=[
            pltpu.HBM((CHIPS, 40, 128), jnp.float32),
            f32(4, 32, 128),
            f32(4, 32, 128),
            *[pltpu.VMEM(table.shape, table.dtype) for table in tables],
        ],
        in_specs=[HBM] * 7,
        out_specs=[HBM] + [VMEM] * 7,
        scratch_shapes=[
            pltpu.VMEM((4, 16, 512), jnp.float32),
            pltpu.VMEM((16, 512), jnp.float32),
            pltpu.VMEM((40, 128), jnp.float32),
            pltpu.VMEM((256, 128), jnp.float32),
            pltpu.SemaphoreType.DMA((CHIPS + 7,)),
        ],
        name="split",
        compiler_params=PARAMS,
    )(*far(density.reshape(4, 16, 512), hamiltonian, *tables))
    mine = lax.all_to_all(copies, "row", 0, 0, axis_index_groups=SAME_CORE, tiled=True)
    other = lax.ppermute(mine, "row", [(i, i ^ 1) for i in range(2 * CHIPS)])

    def swap(block, s):
        return lax.ppermute(block, "hier", [(i, i ^ s) for i in range(PLANES)])

    far_blocks = swap(far_blocks, 4)
    packed = pl.pallas_call(
        pack_kernel,
        out_shape=[f32(2, 32, 128)] * 3,
        in_specs=[VMEM] * 2,
        out_specs=[VMEM] * 3,
        name="pack",
        compiler_params=PARAMS,
    )(*near(near_blocks, far_blocks))
    pairs = [swap(packed[s - 1], s) for s in (3, 2, 1)][::-1]

    bf16 = pltpu.VMEM((512, 512), jnp.bfloat16)
    whole = pltpu.VMEM((32, 8, 128), jnp.float32)
    ints, floats, fields = pl.pallas_call(
        prepare_kernel,
        out_shape=[
            jax.ShapeDtypeStruct((4, EDGES), jnp.int32),
            jax.ShapeDtypeStruct((3, EDGES), jnp.float32),
            f32(3, 64, 128),
        ],
        in_specs=[SMEM] * 4 + [VMEM],
        out_specs=[SMEM] * 2 + [VMEM],
        scratch_shapes=[pltpu.SMEM((EDGES,), jnp.int32)],
        name="prepare",
        compiler_params=PARAMS,
    )(*tables[:4], *near(tables[4]))

    h_high, h_low = pl.pallas_call(
        sites_kernel,
        out_shape=[bf16, bf16],
        in_specs=[VMEM] * 2,
        out_specs=[VMEM] * 2,
        scratch_shapes=[pltpu.VMEM((512, 512), jnp.float32)],
        name="sites",
        compiler_params=PARAMS,
    )(*near(mine, other))

    message = pl.pallas_call(
        rows_kernel,
        out_shape=f32(512, 128),
        in_specs=[ANY] * 2 + [VMEM] * 8,
        out_specs=VMEM,
        scratch_shapes=[
            pltpu.SMEM((4, EDGES), jnp.int32),
            pltpu.SMEM((3, EDGES), jnp.float32),
            pltpu.VMEM((256, 128), jnp.float32),
            *[whole] * 7,
            pltpu.SemaphoreType.DMA((2,)),
        ],
        name="rows",
        compiler_params=PARAMS,
    )(ints, floats, *near(fields, h_high, h_low, near_blocks, far_blocks, *pairs))

    received = lax.all_to_all(
        message.reshape(256, 2, 128), ("row", "hier"), 0, 0, tiled=True
    ).reshape(512, 128)

    message, total = pl.pallas_call(
        columns_kernel,
        out_shape=[f32(256, 128), f32(512, 128)],
        in_specs=[VMEM] * 3,
        out_specs=[VMEM] * 2,
        name="columns",
        compiler_params=PARAMS,
    )(*near(received, h_high, h_low))

    received = lax.all_to_all(
        message.reshape(2 * CHIPS, 8, 128), "row", 0, 0, tiled=True
    ).reshape(256, 128)

    base = pl.pallas_call(
        base_kernel, out_shape=f32(64, 512), in_specs=[VMEM] * 2, out_specs=VMEM, name="base",
        compiler_params=PARAMS,
    )(density.reshape(64, 512), *near(total))
    out = pl.pallas_call(
        finish_kernel,
        out_shape=jax.ShapeDtypeStruct((64, 512), jnp.float32),
        in_specs=[VMEM] * 2,
        out_specs=VMEM,
        name="finish",
        compiler_params=PARAMS,
    )(*near(base, received))
    return out.reshape(2, 2, 16, 512)


def solution(mesh):
    in_specs = (P(None, "hier", "row", None), P("row", None), P(), P(), P(), P(), P())
    out_specs = P(None, "hier", "row", None)
    return jax.shard_map(
        on_device, mesh=mesh, in_specs=in_specs, out_specs=out_specs, check_vma=False
    )
```

```python
import jax
import jax.numpy as jnp
from jax import lax
from jax.experimental import pallas as pl
from jax.experimental.pallas import tpu as pltpu
from jax.sharding import PartitionSpec as P

time_step = 0.25
A1 = time_step
A2 = A1 * time_step / 2
A3 = A2 * time_step / 3

PLANES = 8
CHIPS = 16
SAME_CORE = [list(range(core, 2 * CHIPS, 2)) for core in range(2)]
EDGES = 264


VMEM = pl.BlockSpec(memory_space=pltpu.VMEM)
ANY = pl.BlockSpec(memory_space=pl.ANY)
HBM = pl.BlockSpec(memory_space=pltpu.HBM)
SMEM = pl.BlockSpec(memory_space=pltpu.SMEM)
PARAMS = pltpu.CompilerParams(vmem_limit_bytes=24 << 20)


def f32(*shape):
    return pltpu.VMEM(shape, jnp.float32)


def near(*arrays):
    return [pltpu.with_memory_space_constraint(array, pltpu.VMEM) for array in arrays]


def far(*arrays):
    return [pltpu.with_memory_space_constraint(array, pltpu.HBM) for array in arrays]


def my_plane():
    return lax.axis_index("hier").astype(jnp.int32)


def split_kernel(density, hamiltonian, *refs):
    tables, (copies, near_blocks, far_blocks), held = refs[:5], refs[5:8], refs[8:13]
    rows, own, block, tiles, sems = refs[13:]
    plane = my_plane()
    group = lax.axis_index("row").astype(jnp.int32)
    fetch = pltpu.make_async_copy(density, rows, sems.at[CHIPS])
    fetch_own = pltpu.make_async_copy(hamiltonian, own, sems.at[CHIPS + 1])
    fetch_own.start()
    fetch.start()
    loads = [
        pltpu.make_async_copy(table, place, sems.at[CHIPS + 2 + i])
        for i, (table, place) in enumerate(zip(tables, held))
    ]
    for load in loads:
        load.start()
    fetch_own.wait()
    turned = pltpu.roll(own[...], (512 - 16 * group) & 511, 1)
    lane = lax.broadcasted_iota(jnp.int32, (16, 128), 1)
    block[:16] = jnp.where(lane < 16, 0.5 * turned[:, :128], turned[:, :128])
    block[16:32] = turned[:, 128:256]
    last = 0.5 * turned[:, 256:384]
    lane = lax.broadcasted_iota(jnp.int32, (8, 128), 1)
    block[32:] = jnp.where(lane < 16, last[:8], pltpu.roll(last[8:], 16, 1))
    sends = [pltpu.make_async_copy(block, copies.at[r], sems.at[r]) for r in range(CHIPS)]
    for send in sends:
        send.start()
    fetch.wait()
    for p in range(4):
        for j in range(4):
            tiles[pl.ds(64 * p + 16 * j, 16), :] = rows[p, :, 128 * j : 128 * j + 128]
    for s in range(PLANES):
        first = 2 * (plane ^ s)
        target = far_blocks if s & 4 else near_blocks
        for a in range(2):
            picked = tiles[pl.ds(first + a, 16, stride=16), :]
            for p in range(4):
                target[s & 3, 8 * p + 4 * a : 8 * p + 4 * a + 4, :] = picked[4 * p : 4 * p + 4]
    for wait in sends + loads:
        wait.wait()


def join_symmetric(mine, other, upper):
    lane = lax.broadcasted_iota(jnp.int32, (8, 128), 1)
    even = (lax.axis_index("row") & 1) == 0
    for r in range(2 * CHIPS):
        tile, offset = r // 8, 16 * (r % 8)

        def part(at):
            pair = (mine[r // 2, at : at + 8, :], other[r // 2, at : at + 8, :])
            return jnp.where(even, pair[r % 2], pair[1 - r % 2])

        for half in range(2):
            at = 8 * half
            first = part(at)
            second = part(16 + at)
            last = part(32)
            if offset:
                first = pltpu.roll(first, offset, 1)
                second = pltpu.roll(second, offset, 1)
            if (offset - 16 * half) % 128:
                last = pltpu.roll(last, (offset - 16 * half) % 128, 1)
            last = jnp.where((lane >= offset) & (lane < offset + 16), last, 0.0)
            if offset:
                parts = [
                    jnp.where(lane >= offset, first, 0.0),
                    jnp.where(lane < offset, first, second),
                    jnp.where(lane < offset, second, last),
                ]
            else:
                parts = [first, second, last]
            parts.append(jnp.zeros_like(first))
            for i in range(4):
                col = 128 * ((tile + i) % 4)
                upper[16 * r + at : 16 * r + at + 8, col : col + 128] = parts[i]
    value = upper[...]
    return value + jnp.transpose(value)


def sites_kernel(mine, other, h_high, h_low, upper):
    high, low = halves(join_symmetric(mine, other, upper))
    h_high[...] = high
    h_low[...] = low


def pack_kernel(near_blocks, far_blocks, *out):
    for s in range(1, 4):
        out[s - 1][0] = near_blocks[s]
        out[s - 1][1] = far_blocks[s]


def prepare_kernel(levels, neighbours, decay, bath, couplings, ints, floats, fields, codes):
    plane = my_plane()
    row = 16 * lax.axis_index("row").astype(jnp.int32) + 2 * plane

    def place(g):
        return (plane ^ (g >> 1)) * 4 + (g & 1)

    count = 0
    for m in range(16):
        for k in range(8):
            lower = neighbours[1, k, m]
            codes[count] = lower * 128 + (8 * m + k)
            count = count + (lower >= 0).astype(jnp.int32)
    ints[3, 0] = count

    def unpack(e, carry):
        code = codes[e]
        m = (code >> 3) & 15
        k = code & 7
        level = levels[k, m].astype(jnp.float32)
        ints[0, e] = place(m)
        ints[1, e] = place(code >> 7)
        ints[2, e] = 8 * k
        floats[0, e] = level * bath[1, k]
        floats[1, e] = level * bath[0, k]
        return carry

    lax.fori_loop(0, count, unpack, 0)
    for m in range(16):
        total = levels[0, m].astype(jnp.float32) * decay[0]
        for k in range(1, 8):
            total = total + levels[k, m].astype(jnp.float32) * decay[k]
        floats[2, place(m)] = total

    values = couplings[...]
    lane = lax.broadcasted_iota(jnp.int32, values.shape, 1)
    for a in range(2):
        own = jnp.sum(jnp.where(lane == row + a, values, 0.0), axis=1, keepdims=True)
        own = jnp.broadcast_to(own, (8, 128))
        for j in range(4):
            here = pl.ds(4 * a + j, 8, stride=8)
            there = values[:, 128 * j : 128 * j + 128]
            fields[0, here, :] = own - there
            fields[1, here, :] = own + there
            fields[2, here, :] = there


def mix(ints, floats, fields, *jobs):
    def step(e, carry):
        m = ints[0, e]
        q = ints[1, e]
        k = pl.multiple_of(ints[2, e], 8)
        even = floats[0, e]
        odd = floats[1, e]
        d = fields[0, pl.ds(k, 8), :]
        f = odd * d
        g = even * fields[1, pl.ds(k, 8), :]
        for source, both, right in jobs:
            xm, ym = source[m], source[m + 2]
            xq, yq = source[q], source[q + 2]
            both[m] = both[m] + (g * xq + f * yq)
            both[m + 2] = both[m + 2] + (g * yq - f * xq)
            both[q] = both[q] + d * ym
            both[q + 2] = both[q + 2] - d * xm
            if right is not None:
                c = fields[2, pl.ds(k, 8), :]
                gr = even * c
                fr = odd * c
                right[m] = right[m] + (gr * xq - fr * yq)
                right[m + 2] = right[m + 2] + (gr * yq + fr * xq)
                right[q] = right[q] - c * ym
                right[q + 2] = right[q + 2] + c * xm
        return carry

    lax.fori_loop(0, ints[3, 0], step, 0)


def decayed(floats, source):
    parts = []
    for s in range(PLANES):
        for part in range(2):
            for m in range(2):
                parts.append((-floats[2, 4 * s + m]) * source[4 * s + 2 * part + m])
    return jnp.stack(parts)


def gather_rows(ref):
    return jnp.concatenate(
        [
            jnp.concatenate([ref[pl.ds(4 * a + j, 32, stride=8), :] for j in range(4)], axis=1)
            for a in range(2)
        ],
        axis=0,
    )


def spread_rows(ref, value):
    for a in range(2):
        for j in range(4):
            ref[pl.ds(4 * a + j, 32, stride=8), :] = value[
                32 * a : 32 * a + 32, 128 * j : 128 * j + 128
            ]


def halves(value):
    high = value.astype(jnp.bfloat16)
    low = (value - high.astype(jnp.float32)).astype(jnp.bfloat16)
    return high, low


def times_i(value):
    value = value.reshape(PLANES, 2, 2, 8, 128)
    return jnp.concatenate([-value[:, 1:], value[:, :1]], axis=1).reshape(32, 8, 128)


def swap_blocks(value):
    lead = value.shape[0]
    block = lax.broadcasted_iota(jnp.int32, (8, 128), 1) // 16
    for k in range(3):
        width = 16 << k
        low = ((block >> k) & 1) == 0
        pairs = value.reshape(lead, 4 >> k, 2, 1 << k, 8, 128)
        zero, one = pairs[:, :, 0], pairs[:, :, 1]
        shape = zero.shape
        zero = zero.reshape(-1, 128)
        one = one.reshape(-1, 128)
        up = pltpu.roll(one, width, 1)
        down = pltpu.roll(zero, 128 - width, 1)
        low = jnp.broadcast_to(low[None], (zero.shape[0] // 8, 8, 128)).reshape(-1, 128)
        new_zero = jnp.where(low, zero, up).reshape(shape)
        new_one = jnp.where(low, down, one).reshape(shape)
        value = jnp.stack([new_zero, new_one], axis=2).reshape(lead, 8, 8, 128)
    return value


def rows_kernel(ints_far, floats_far, fields, h_high, h_low, near_blocks, far_blocks, *refs):
    *pairs, message, ints, floats, rows, state, first, right, second, p, ep, bp, sems = refs
    plane = my_plane()
    fetches = [
        pltpu.make_async_copy(ints_far, ints, sems.at[0]),
        pltpu.make_async_copy(floats_far, floats, sems.at[1]),
    ]
    for fetch in fetches:
        fetch.start()
    state[0:4] = near_blocks[0].reshape(4, 8, 128)
    state[16:20] = far_blocks[0].reshape(4, 8, 128)
    for s in range(1, 4):
        state[4 * s : 4 * s + 4] = pairs[s - 1][0].reshape(4, 8, 128)
        state[4 * s + 16 : 4 * s + 20] = pairs[s - 1][1].reshape(4, 8, 128)
    right[...] = jnp.zeros_like(right)
    high, low = h_high[...], h_low[...]

    def product(value):
        count = value.shape[0]
        value_high, value_low = halves(value)
        main = jnp.dot(
            jnp.concatenate([value_high, value_low], axis=0),
            high,
            preferred_element_type=jnp.float32,
        )
        rest = jnp.dot(value_high, low, preferred_element_type=jnp.float32)
        return main[:count] + main[count:] + rest

    def apply(values):
        stacked = []
        for value in values:
            rows[...] = value.reshape(256, 128)
            stacked.append(gather_rows(rows))
        result = product(jnp.concatenate(stacked, axis=0))
        out = []
        for i in range(len(values)):
            spread_rows(rows, result[64 * i : 64 * i + 64])
            out.append(times_i(rows[...].reshape(32, 8, 128)))
        return out

    s_value = state[...]
    (p_value,) = apply([s_value])
    p[...] = p_value
    for fetch in fetches:
        fetch.wait()
    first[...] = decayed(floats, state)
    mix(ints, floats, fields, (state, first, right))
    first[...] = A2 * state[...] + A3 * first[...]
    second[...] = decayed(floats, first)
    v1, edge = apply([first[...] + A3 * p_value, p_value + right[...]])
    damped = decayed(floats, p)
    ep[...] = damped
    bp[...] = damped + edge
    mix(ints, floats, fields, (p, ep, bp), (first, second, None))
    k_value = A2 * p_value + 3 * A3 * bp[...]
    z_value = 0.5 * A1 * s_value + v1 + A3 * ep[...] + 0.5 * second[...]
    v2 = z_value + 0.5 * A1 * s_value + 0.5 * second[...]
    (g_value,) = apply([v2])
    p[...] = z_value
    ep[...] = g_value + decayed(floats, p)
    mix(ints, floats, fields, (p, ep, None))
    both = jnp.concatenate(
        [k_value.reshape(8, 4, 8, 128), ep[...].reshape(8, 4, 8, 128)], axis=1
    )
    both = swap_blocks(both)
    for s in range(PLANES):
        start = 2 * (plane ^ s)
        for b in range(8):
            for a in range(2):
                message[pl.ds(start + 16 * b + a, 4, stride=128), :] = both[
                    s, b, 4 * a : 4 * a + 4, :
                ]


def columns_kernel(received, h_high, h_low, message, total):
    value = received[...]
    high, low = halves(value)
    main = jnp.dot(
        h_high[...], jnp.concatenate([high, low], axis=1), preferred_element_type=jnp.float32
    )
    rest = jnp.dot(h_low[...], high, preferred_element_type=jnp.float32)
    z = main[:, :128] + main[:, 128:] + rest
    lane = lax.broadcasted_iota(jnp.int32, z.shape, 1)
    other = pltpu.roll(value, 64, 1)
    result = jnp.where(
        lane < 32, pltpu.roll(z, 96, 1) + other, pltpu.roll(z, 32, 1) - other
    )
    total[...] = result
    tiles = result.reshape(32, 2, 8, 128)
    upper = pltpu.roll(tiles[:, 1].reshape(256, 128), 64, 1)
    lane = lax.broadcasted_iota(jnp.int32, upper.shape, 1)
    message[...] = jnp.where(lane < 64, tiles[:, 0].reshape(256, 128), upper)


def finish_kernel(density, total, received, out):
    value = swap_blocks(received[...].reshape(4, 8, 8, 128))
    base = density[...] + jnp.transpose(total[...])[:64]
    for g in range(4):
        for half in range(2):
            for p in range(4):
                row = slice(16 * p + 8 * half, 16 * p + 8 * half + 8)
                col = slice(128 * g, 128 * g + 128)
                part = value[g, 4 * half + p]
                out[row, col] = base[row, col] + part if p < 2 else base[row, col] - part


def on_device(density, hamiltonian, couplings, decay_rates, bath_coeffs, levels, neighbours):
    tables = (levels.T, jnp.swapaxes(neighbours, 1, 2), decay_rates, bath_coeffs, couplings)
    copies, near_blocks, far_blocks, *tables = pl.pallas_call(
        split_kernel,
        out_shape=[
            pltpu.HBM((CHIPS, 40, 128), jnp.float32),
            f32(4, 32, 128),
            f32(4, 32, 128),
            *[pltpu.VMEM(table.shape, table.dtype) for table in tables],
        ],
        in_specs=[HBM] * 7,
        out_specs=[HBM] + [VMEM] * 7,
        scratch_shapes=[
            pltpu.VMEM((4, 16, 512), jnp.float32),
            pltpu.VMEM((16, 512), jnp.float32),
            pltpu.VMEM((40, 128), jnp.float32),
            pltpu.VMEM((256, 128), jnp.float32),
            pltpu.SemaphoreType.DMA((CHIPS + 7,)),
        ],
        name="split",
        compiler_params=PARAMS,
    )(*far(density.reshape(4, 16, 512), hamiltonian, *tables))
    mine = lax.all_to_all(copies, "row", 0, 0, axis_index_groups=SAME_CORE, tiled=True)
    other = lax.ppermute(mine, "row", [(i, i ^ 1) for i in range(2 * CHIPS)])

    def swap(block, s):
        return lax.ppermute(block, "hier", [(i, i ^ s) for i in range(PLANES)])

    far_blocks = swap(far_blocks, 4)
    packed = pl.pallas_call(
        pack_kernel,
        out_shape=[f32(2, 32, 128)] * 3,
        in_specs=[VMEM] * 2,
        out_specs=[VMEM] * 3,
        name="pack",
        compiler_params=PARAMS,
    )(*near(near_blocks, far_blocks))
    pairs = [swap(packed[s - 1], s) for s in (3, 2, 1)][::-1]

    bf16 = pltpu.VMEM((512, 512), jnp.bfloat16)
    whole = pltpu.VMEM((32, 8, 128), jnp.float32)
    ints, floats, fields = pl.pallas_call(
        prepare_kernel,
        out_shape=[
            jax.ShapeDtypeStruct((4, EDGES), jnp.int32),
            jax.ShapeDtypeStruct((3, EDGES), jnp.float32),
            f32(3, 64, 128),
        ],
        in_specs=[SMEM] * 4 + [VMEM],
        out_specs=[SMEM] * 2 + [VMEM],
        scratch_shapes=[pltpu.SMEM((EDGES,), jnp.int32)],
        name="prepare",
        compiler_params=PARAMS,
    )(*tables[:4], *near(tables[4]))

    h_high, h_low = pl.pallas_call(
        sites_kernel,
        out_shape=[bf16, bf16],
        in_specs=[VMEM] * 2,
        out_specs=[VMEM] * 2,
        scratch_shapes=[pltpu.VMEM((512, 512), jnp.float32)],
        name="sites",
        compiler_params=PARAMS,
    )(*near(mine, other))

    message = pl.pallas_call(
        rows_kernel,
        out_shape=f32(512, 128),
        in_specs=[ANY] * 2 + [VMEM] * 8,
        out_specs=VMEM,
        scratch_shapes=[
            pltpu.SMEM((4, EDGES), jnp.int32),
            pltpu.SMEM((3, EDGES), jnp.float32),
            pltpu.VMEM((256, 128), jnp.float32),
            *[whole] * 7,
            pltpu.SemaphoreType.DMA((2,)),
        ],
        name="rows",
        compiler_params=PARAMS,
    )(ints, floats, *near(fields, h_high, h_low, near_blocks, far_blocks, *pairs))

    received = lax.all_to_all(
        message.reshape(256, 2, 128), ("row", "hier"), 0, 0, tiled=True
    ).reshape(512, 128)

    message, total = pl.pallas_call(
        columns_kernel,
        out_shape=[f32(256, 128), f32(512, 128)],
        in_specs=[VMEM] * 3,
        out_specs=[VMEM] * 2,
        name="columns",
        compiler_params=PARAMS,
    )(*near(received, h_high, h_low))

    received = lax.all_to_all(
        message.reshape(2 * CHIPS, 8, 128), "row", 0, 0, tiled=True
    ).reshape(256, 128)

    out = pl.pallas_call(
        finish_kernel,
        out_shape=jax.ShapeDtypeStruct((64, 512), jnp.float32),
        in_specs=[VMEM] * 3,
        out_specs=VMEM,
        name="finish",
        compiler_params=PARAMS,
    )(*near(density.reshape(64, 512), total, received))
    return out.reshape(2, 2, 16, 512)


def solution(mesh):
    in_specs = (P(None, "hier", "row", None), P("row", None), P(), P(), P(), P(), P())
    out_specs = P(None, "hier", "row", None)
    return jax.shard_map(
        on_device, mesh=mesh, in_specs=in_specs, out_specs=out_specs, check_vma=False
    )
```
